32 devices in a mesh: dp: 8 (over y, x, core), tensor: 4 (over z).
Axes of the slice: x: 2, y: 2, z: 4, core: 2. Of those that a mesh axis runs over, the one named last changes fastest.
Arguments:
- hidden_in: bfloat16 [2048, 8192], P('dp'), may hold values from -6 to 6
- queries: bfloat16 [2048, 8192], P('dp', 'tensor'), may hold values from -8 to 8
- keys: bfloat16 [2048, 1024], P('dp', 'tensor'), may hold values from -8 to 8
- value_weight: bfloat16 [8192, 1024], P('dp', 'tensor'), may hold values from -0.0625 to 0.0625
- context_grad: bfloat16 [2048, 8192], P('dp', 'tensor'), may hold values from -6 to 6
- doc_ids: int32 [8, 256], P('dp'), may hold values from 0 to 15, never falling along the last dimension, each value on 1 to 128 neighbouring positions
- token_counts: int32 [8], P('dp'), may hold values from 64 to 256, as said below
Outputs:
- context: bfloat16 [2048, 8192], P('dp', 'tensor')
- w_value_grad: float32 [8192, 1024], P('dp', 'tensor')
The draws below stay inside these ranges and needn't reach their ends.
Inputs may be any that keep to these rules, and one draw needn't show every extreme that they name: `token_counts`: every replica has at least 64 tokens with a loss, and some replica has all 256; its other rows are padding. `doc_ids`: within a replica documents are numbered in order; a document has 1 to 128 tokens.
All inputs are finite; a program needn't handle non-finite values.
Results may differ from the reference program's by a relative error of at most 0.0054.
Values may be sent and summed in bfloat16 or wider, within the bound.
A program may use at most 64 MiB of HBM per device.

```python
import math
import jax
import jax.numpy as jnp
import numpy as np
from jax import lax

MODEL_WIDTH = 8192
QUERY_HEADS = 64
KEY_VALUE_HEADS = 8
HEAD_SIZE = 128
REPLICA_TOKENS = 256
TOKENS = 2048
N_DP = 8


def unmasked_rows(key, cols):
    return jnp.clip(jax.random.normal(key, (TOKENS, cols), jnp.float32), -6.0, 6.0)


def draw_queries(key, part):
    base_offset = unmasked_rows(jax.random.fold_in(key, 21), QUERY_HEADS * HEAD_SIZE)
    return base_offset.astype(jnp.bfloat16)


def draw_keys(key, part):
    base_offset = unmasked_rows(jax.random.fold_in(key, 31), KEY_VALUE_HEADS * HEAD_SIZE)
    return base_offset.astype(jnp.bfloat16)


def draw_token_counts(key, part):
    replica = jnp.arange(N_DP, dtype=jnp.int32)
    base_offset = REPLICA_TOKENS // 4 + replica * (REPLICA_TOKENS // 2) // max(N_DP - 1, 1)
    extra = jax.random.randint(jax.random.fold_in(key, 41), (N_DP,), 0, REPLICA_TOKENS // 4 + 1)
    chosen = jax.random.randint(jax.random.fold_in(key, 43), (), 0, N_DP)
    counts = jnp.minimum(base_offset + extra, REPLICA_TOKENS)
    return jnp.where(replica == chosen, REPLICA_TOKENS, counts).astype(jnp.int32)


def with_spikes(drawn, own_key, source, target, parts, factor):
    owner, partner = [(jnp.arange(drawn.shape[dim]) // (drawn.shape[dim] // parts)).reshape([-1 if axis == dim else 1 for axis in range(drawn.ndim)]) for dim in (source, target)]
    chosen = jax.random.permutation(own_key, parts)[partner]
    strong = (owner == chosen) | (owner == (partner + parts // 2) % parts)
    return jnp.where(strong, factor * drawn, drawn)


def block_scale(stream_key, extent, shards, low, largest):
    def one(dim, blocks):
        heights = jax.random.uniform(jax.random.fold_in(jax.random.fold_in(stream_key, 6), dim), (blocks,), jnp.float32, low / len(shards), largest / len(shards))
        return jnp.repeat(jnp.exp(heights), extent[dim] // blocks).reshape((-1,) + (1,) * (len(extent) - dim - 1))

    level = one(*shards[0])
    for cut in shards[1:]:
        level = level * one(*cut)
    return level


def profile(count, total, limit, skew):
    portions = [(1 << 20) // math.isqrt(standing ** skew) + 1 for standing in range(2, count + 1)]
    spare, given = total - limit - (count - 1), [1] * (count - 1)
    while spare > 0:
        candidates = [i for i in range(count - 1) if given[i] < limit]
        whole, left = sum([portions[i] for i in candidates]), spare
        for i in candidates:
            addition = min(limit - given[i], max(1, left * portions[i] // whole), spare)
            given[i] = given[i] + addition
            spare = spare - addition
    return np.array([limit] + given)


def ragged(key, count, total, limit, slope):
    if count == 2:
        one = jax.random.randint(key, (), max(1, total - limit), min(limit, total - 1) + 1)
        return jnp.stack([one, total - one])
    tallies = jnp.asarray(profile(count, total, limit, slope), jnp.int32)
    couples = (count - 1) // 2
    giver, taker = tallies[1:1 + 2 * couples:2], tallies[2:2 + 2 * couples:2]
    slack = jnp.minimum(giver - 1, limit - taker)
    moved = jax.random.randint(jax.random.fold_in(key, 1), (couples,), 0, 1 << 20) % (slack + 1)
    tallies = tallies.at[1:1 + 2 * couples:2].set(giver - moved).at[2:2 + 2 * couples:2].set(taker + moved)
    return tallies[jax.random.permutation(jax.random.fold_in(key, 2), count)]


def centred(key, shape, scale, bound, pieces=(), kind=jnp.bfloat16):
    array = scale * jax.random.normal(key, shape, jnp.float32)
    if pieces:
        array = array * block_scale(key, shape, pieces, -0.22, 0.18)
    return jnp.clip(array, -bound, bound).astype(kind)


def heavy_noise(own_key, shape, deviation, bound, cuts, heavy, kind=jnp.bfloat16):
    result = deviation * jax.random.normal(own_key, shape, jnp.float32)
    if cuts:
        result = result * block_scale(own_key, shape, cuts, -0.22, 0.18)
    return jnp.clip(with_spikes(result, jax.random.fold_in(own_key, 3), *heavy), -bound, bound).astype(kind)


def setup_inputs(seed: int = 0) -> dict:
    streams_of = jax.random.split(jax.random.key(seed), 8)
    return {
        "hidden_in": heavy_noise(streams_of[0], (TOKENS, MODEL_WIDTH), 1.0, 6.0, ((0, 8),), (0, 1, 8, 2.0)),
        "queries": draw_queries(jax.random.fold_in(streams_of[7], 71), 0),
        "keys": draw_keys(jax.random.fold_in(streams_of[7], 71), 0),
        "value_weight": centred(streams_of[3], (MODEL_WIDTH, KEY_VALUE_HEADS * HEAD_SIZE), MODEL_WIDTH ** -0.5, 0.0625, ((0, 8), (1, 4))),
        "context_grad": centred(streams_of[4], (TOKENS, QUERY_HEADS * HEAD_SIZE), 1.0, 6.0, ((0, 8), (1, 4))),
        "doc_ids": jax.vmap(lambda own: jnp.searchsorted(jnp.cumsum(ragged(own, REPLICA_TOKENS // 16, REPLICA_TOKENS, REPLICA_TOKENS // 2, 2)), jnp.arange(REPLICA_TOKENS), side="right"))(jax.random.split(streams_of[5], N_DP)).reshape((N_DP, REPLICA_TOKENS)).astype(jnp.int32),
        "token_counts": draw_token_counts(jax.random.fold_in(streams_of[7], 71), 0),
    }


def reference(hidden_in, queries, keys, value_weight, context_grad, doc_ids, token_counts):
    query_group = QUERY_HEADS // KEY_VALUE_HEADS
    scale = 1.0 / math.sqrt(HEAD_SIZE)
    counts_f = token_counts.astype(jnp.float32)
    total = jnp.sum(counts_f)
    x_rep = hidden_in.reshape(N_DP, REPLICA_TOKENS, MODEL_WIDTH)
    q_rep = queries.reshape(N_DP, REPLICA_TOKENS, QUERY_HEADS * HEAD_SIZE)
    key_repeated = keys.reshape(N_DP, REPLICA_TOKENS, KEY_VALUE_HEADS * HEAD_SIZE)
    g_rep = context_grad.reshape(N_DP, REPLICA_TOKENS, QUERY_HEADS * HEAD_SIZE)
    position = jnp.arange(REPLICA_TOKENS, dtype=jnp.int32)

    def replica(acc, item):
        x_here, query_local, key_local, g_here, doc_here, count_here = item
        value_states = jnp.dot(x_here, value_weight, preferred_element_type=jnp.float32).astype(jnp.bfloat16)
        query_four_axes = query_local.reshape(REPLICA_TOKENS, KEY_VALUE_HEADS, query_group, HEAD_SIZE).astype(jnp.float32)
        key_three_axes = key_local.reshape(REPLICA_TOKENS, KEY_VALUE_HEADS, HEAD_SIZE).astype(jnp.float32)
        scores = jnp.einsum('ikgd,jkd->kgij', query_four_axes, key_three_axes) * scale
        allowed = (position[None, :] <= position[:, None]) & (doc_here[:, None] == doc_here[None, :])
        scores = jnp.where(allowed, scores, -jnp.inf)
        top = lax.optimization_barrier(jnp.max(scores, axis=-1, keepdims=True))
        expo = jnp.exp(scores - top)
        probs = (expo / lax.optimization_barrier(jnp.sum(expo, axis=-1, keepdims=True))).astype(jnp.bfloat16)
        value_three_axes = value_states.reshape(REPLICA_TOKENS, KEY_VALUE_HEADS, HEAD_SIZE).astype(jnp.float32)
        ctx = jnp.einsum('kgij,jkd->ikgd', probs.astype(jnp.float32), value_three_axes)
        ctx = ctx.astype(jnp.bfloat16).reshape(REPLICA_TOKENS, QUERY_HEADS * HEAD_SIZE)
        valid = position < count_here
        masked_scores = jnp.where(valid[:, None], g_here, jnp.zeros_like(g_here))
        masked_scores = masked_scores.reshape(REPLICA_TOKENS, KEY_VALUE_HEADS, query_group, HEAD_SIZE).astype(jnp.float32)
        value_gradient = jnp.einsum('kgij,ikgd->jkd', probs.astype(jnp.float32), masked_scores)
        value_gradient = value_gradient.astype(jnp.bfloat16).reshape(REPLICA_TOKENS, KEY_VALUE_HEADS * HEAD_SIZE)
        term = jnp.dot(x_here.T, value_gradient, preferred_element_type=jnp.float32)
        return (acc + term * count_here.astype(jnp.float32), ctx)
    start_index = jnp.zeros((MODEL_WIDTH, KEY_VALUE_HEADS * HEAD_SIZE), jnp.float32)
    acc, ctx_all = lax.scan(replica, start_index, (x_rep, q_rep, key_repeated, g_rep, doc_ids, token_counts))
    return (ctx_all.reshape(TOKENS, QUERY_HEADS * HEAD_SIZE), acc / total)
```

```python
import functools
import math

import jax
import jax.numpy as jnp
from jax import lax
from jax.experimental import pallas as pl
from jax.experimental.pallas import tpu as pltpu
from jax.sharding import PartitionSpec as P

QUERY_HEADS = 64
KEY_VALUE_HEADS = 8
HEAD_SIZE = 128
GROUP = QUERY_HEADS // KEY_VALUE_HEADS
PIECE = 64
MESH = pl.DeviceIdType.MESH
F32 = jnp.float32
BF16 = jnp.bfloat16


def plain(hidden_in, queries, keys, value_weight, context_grad, doc_ids, token_counts):
    tok_rows = hidden_in.shape[0]
    kv_cols = keys.shape[1]
    kv_local = kv_cols // HEAD_SIZE
    scale = 1.0 / math.sqrt(HEAD_SIZE)
    whole = lax.all_gather(value_weight, "dp", axis=0, tiled=True)
    value_states = jnp.dot(hidden_in, whole, preferred_element_type=F32).astype(BF16)
    query_four_axes = queries.reshape(tok_rows, kv_local, GROUP, HEAD_SIZE)
    key_three_axes = keys.reshape(tok_rows, kv_local, HEAD_SIZE)
    scores = (
        jnp.einsum("ikgd,jkd->kgij", query_four_axes, key_three_axes, preferred_element_type=F32)
        * scale
    )
    position = jnp.arange(tok_rows, dtype=jnp.int32)
    doc_here = doc_ids[0]
    allowed = (position[None, :] <= position[:, None]) & (doc_here[:, None] == doc_here[None, :])
    scores = jnp.where(allowed, scores, -jnp.inf)
    top = jnp.max(scores, axis=-1, keepdims=True)
    expo = jnp.exp(scores - top)
    probs = (expo / jnp.sum(expo, axis=-1, keepdims=True)).astype(BF16)
    value_three_axes = value_states.reshape(tok_rows, kv_local, HEAD_SIZE)
    ctx = jnp.einsum("kgij,jkd->ikgd", probs, value_three_axes, preferred_element_type=F32)
    context = ctx.astype(BF16).reshape(tok_rows, kv_local * GROUP * HEAD_SIZE)
    count_here = token_counts[0]
    valid = position < count_here
    masked = jnp.where(valid[:, None], context_grad, jnp.zeros_like(context_grad))
    masked = masked.reshape(tok_rows, kv_local, GROUP, HEAD_SIZE)
    value_gradient = jnp.einsum("kgij,ikgd->jkd", probs, masked, preferred_element_type=F32)
    value_gradient = value_gradient.astype(BF16).reshape(tok_rows, kv_cols)
    count_float = count_here.astype(F32)
    factor = count_float / lax.psum(count_float, "dp")
    full_term = (
        jnp.einsum("tr,tc->rc", hidden_in, value_gradient, preferred_element_type=F32) * factor
    )
    grad = lax.psum_scatter(full_term, "dp", scatter_dimension=0, tiled=True)
    return (context, grad)


def dot_tt(a, b):
    return lax.dot_general(a, b, (((0,), (0,)), ((), ())), preferred_element_type=F32)


def fused_kernel(
    x_hbm, q_hbm, k_hbm, w_hbm, g_hbm, doc_hbm, cnt_ref, ctx, dw_ref,
    x, xp, q, k, g, wg, pt, bias, dv, dvp, dvn, xn, vown, vsend, vrecv, pf, pfr, ps, pr,
    sendbuf, recvbuf, acc, cnts, doc_ref,
    lsem, xs, xr, ws, wr, cs, cr, ds, dr, vs, vr, ss, sr, ns, nr, zs, zr, fs, fr, qs, qr,
):
    me = lax.axis_index("dp")
    plane = lax.axis_index("tensor")
    planes = xn.shape[2] // PIECE
    core = lax.rem(me, 2)
    chip = me // 2
    cx = lax.rem(chip, 2)
    cy = chip // 2
    peer = me + 1 - 2 * core
    T, C = k.shape
    R = w_hbm.shape[0]
    H = R // 2
    kv = C // HEAD_SIZE
    scale = 1.0 / math.sqrt(HEAD_SIZE)

    def chip_at(rel):
        ax = 1 - cx if rel % 2 else cx
        ay = 1 - cy if rel // 2 else cy
        return 2 * ay + ax

    def same(rel):
        return 2 * chip_at(rel) + core

    def cross(rel):
        return 2 * chip_at(rel) + 1 - core

    lk = pltpu.make_async_copy(k_hbm, k, lsem.at[0])
    lq = pltpu.make_async_copy(q_hbm, q, lsem.at[1])
    lg = pltpu.make_async_copy(g_hbm, g, lsem.at[2])
    lx = pltpu.make_async_copy(x_hbm, x, lsem.at[3])
    lw = pltpu.make_async_copy(w_hbm, wg.at[0], lsem.at[4])
    ld = pltpu.make_async_copy(doc_hbm, doc_ref, lsem.at[5])
    for c in (ld, lk, lq, lg, lx, lw):
        c.start()

    bar = pltpu.get_barrier_semaphore()
    others = (peer, same(1), same(2), cross(1), cross(2))
    for d in others:
        pl.semaphore_signal(bar, inc=1, device_id={"dp": d}, device_id_type=MESH)

    @pl.when(plane > 0)
    def _():
        pl.semaphore_signal(bar, inc=1, device_id={"tensor": plane - 1}, device_id_type=MESH)

    @pl.when(plane < planes - 1)
    def _():
        pl.semaphore_signal(bar, inc=1, device_id={"tensor": plane + 1}, device_id_type=MESH)

    inner = (plane > 0) & (plane < planes - 1)
    pl.semaphore_wait(bar, len(others) + 1 + inner.astype(jnp.int32))

    def remote(src, dst, s, r, dev):
        c = pltpu.make_async_remote_copy(
            src_ref=src, dst_ref=dst, send_sem=s, recv_sem=r,
            device_id={"dp": dev}, device_id_type=MESH,
        )
        c.start()
        return c

    half = (pl.ds(0, H), pl.ds(H, H))
    near = (1, 2)
    sends = []

    rows = pl.ds(pl.multiple_of(plane * PIECE, PIECE), PIECE)
    for a in (0, 1):
        n = near[a]
        for other in (0, 1):
            dev = cross(n) if other else same(n)
            cols = pl.ds(pl.multiple_of(dev * R + a * H, H), H)
            i = 2 * a + other
            sends.append(
                remote(x_hbm.at[rows, cols], xn.at[a, other, rows, :], ns.at[i], nr.at[i], dev)
            )
    direct = list(sends)

    def own_half(rel, part):
        i = part
        return remote(
            w_hbm.at[half[part]], wg.at[rel, half[part]], ws.at[i], wr.at[i], same(rel)
        )

    def onward(src, part):
        i = 2 + part
        return remote(
            wg.at[src, half[part]], wg.at[3, half[part]], ws.at[i], wr.at[i], same(3 - src)
        )

    wx1, wy0 = own_half(1, 1), own_half(2, 0)
    count = cnt_ref[0].astype(F32)
    cnts[0] = jnp.full(cnts.shape[1:], count, F32)
    c0 = remote(cnts.at[0], cnts.at[1], cs.at[0], cr.at[0], peer)
    xcopies = []
    for i, (rel, part) in enumerate(((3, None), (0, None), (1, 1), (2, 0))):
        first = cross(rel) * R
        if part is None:
            src = x_hbm.at[:, pl.ds(pl.multiple_of(first, R), R)]
            dst = xp.at[rel]
        else:
            src = x_hbm.at[:, pl.ds(pl.multiple_of(first + part * H, H), H)]
            dst = xp.at[rel, :, half[part]]
        xcopies.append(remote(src, dst, xs.at[i], xr.at[i], peer))

    def zcopy(a, piece, to, slot):
        rows = pl.ds(pl.multiple_of(piece * PIECE, PIECE), PIECE)
        return pltpu.make_async_remote_copy(
            src_ref=xn.at[a, :, rows, :], dst_ref=xn.at[a, :, rows, :],
            send_sem=zs.at[a, slot], recv_sem=zr.at[a, piece],
            device_id={"tensor": to}, device_id_type=MESH,
        )

    def zmoves(step):
        down, up = plane + step, plane - step
        return (
            (down, plane - 1, (plane > 0) & (down < planes), 2 * step),
            (up, plane + 1, (plane < planes - 1) & (up >= 0), 2 * step + 1),
        )

    def zwait(a, piece):
        zcopy(a, piece, plane, 0).wait_recv()

    def zstep(step):
        for a in (0, 1):
            for piece, to, has, slot in zmoves(step):
                if step:
                    got = (piece >= 0) & (piece < planes)

                    @pl.when(got)
                    def _(a=a, piece=piece):
                        zwait(a, piece)

                @pl.when(has)
                def _(a=a, piece=piece, to=to, slot=slot):
                    zcopy(a, piece, to, slot).start()

    def zlast():
        for a in (0, 1):
            for piece, to, has, slot in zmoves(planes - 1):
                @pl.when((piece >= 0) & (piece < planes))
                def _(a=a, piece=piece):
                    zwait(a, piece)

    def zsent():
        for step in range(planes - 1):
            for a in (0, 1):
                for piece, to, has, slot in zmoves(step):
                    @pl.when(has)
                    def _(a=a, piece=piece, to=to, slot=slot):
                        zcopy(a, piece, to, slot).wait_send()

    ld.wait()
    docs = jnp.broadcast_to(doc_ref[...].astype(F32), (T, T))
    jj = lax.broadcasted_iota(jnp.int32, (T, T), 0)
    ii = lax.broadcasted_iota(jnp.int32, (T, T), 1)
    allowed = (jj <= ii) & (docs == docs.T)
    bias[...] = jnp.where(allowed, 0.0, -jnp.inf).astype(F32)
    lk.wait()
    lq.wait()
    lg.wait()
    row = lax.broadcasted_iota(jnp.int32, (T, HEAD_SIZE), 0).astype(F32)

    def group(kh, _):
        kcols = pl.ds(pl.multiple_of(kh * HEAD_SIZE, HEAD_SIZE), HEAD_SIZE)
        keyg = k[:, kcols]
        total = jnp.zeros((T, HEAD_SIZE), F32)
        for h in range(GROUP):
            cols = pl.ds(pl.multiple_of((kh * GROUP + h) * HEAD_SIZE, HEAD_SIZE), HEAD_SIZE)
            st = lax.dot_general(
                keyg, q[:, cols], (((1,), (1,)), ((), ())), preferred_element_type=F32
            )
            st = st * scale + bias[...]
            e = jnp.exp(st - jnp.max(st, axis=0, keepdims=True))
            p = (e * (1.0 / jnp.sum(e, axis=0, keepdims=True))).astype(BF16)
            pt[kh * GROUP + h] = p
            gm = jnp.where(row < count, g[:, cols].astype(F32), 0.0).astype(BF16)
            total = total + jnp.dot(p, gm, preferred_element_type=F32)
        dv[:, kcols] = (total * count).astype(BF16)
        return 0

    split = kv // 2
    lax.fori_loop(0, split, group, 0)
    for c in direct:
        c.wait_recv()
    zstep(0)
    c0.wait_recv()
    cnts[2] = cnts[0] + cnts[1]
    c1 = remote(cnts.at[2], cnts.at[3], cs.at[1], cr.at[1], same(1))
    lax.fori_loop(split, kv, group, 0)
    dcopies = [
        remote(dv, dvp, ds.at[0], dr.at[0], peer),
        remote(dv, dvn.at[0, 0], ds.at[1], dr.at[1], same(1)),
        remote(dv, dvn.at[1, 0], ds.at[2], dr.at[2], same(2)),
    ]
    lx.wait()
    for c in xcopies:
        c.wait_recv()
    dcopies[0].wait_recv()
    step = min(256, H)

    def partial(rel, part, store):
        base = same(rel) * R
        first = part * H

        def body(t, _):
            off = pl.multiple_of(first + t * step, step)
            xa = x[:, pl.ds(pl.multiple_of(base + off, step), step)]
            xb = xp[rel, :, pl.ds(off, step)]
            store(off, dot_tt(xa, dv[...]) + dot_tt(xb, dvp[...]))
            return 0

        lax.fori_loop(0, H // step, body, 0)

    def ship(slot, rel, part, to, add=None):
        def put(off, val):
            here = pl.ds(off - part * H, step)
            if add is not None:
                val = val + recvbuf[add, here, :].astype(F32)
            sendbuf[slot, here, :] = val.astype(BF16)

        partial(rel, part, put)
        return remote(sendbuf.at[slot], recvbuf.at[slot], ss.at[slot], sr.at[slot], same(to))

    def keep(off, val):
        acc[pl.ds(off, step), :] = val

    scopies = [ship(0, 3, 0, 1), ship(1, 3, 1, 2)]
    wx1.wait_recv()
    fx1 = onward(1, 1)
    wy0.wait_recv()
    fy0 = onward(2, 0)
    zstep(1)
    c1.wait_recv()
    cnts[4] = cnts[2] + cnts[3]
    c2 = remote(cnts.at[4], cnts.at[5], cs.at[2], cr.at[2], same(2))
    for a in (0, 1):
        dcopies[1 + a].wait_recv()
        dcopies.append(
            remote(dvn.at[a, 0], dvn.at[a, 1], ds.at[3 + a], dr.at[3 + a], peer)
        )
    partial(0, 0, keep)
    partial(0, 1, keep)
    scopies[0].wait_recv()
    scopies.append(ship(2, 2, 0, 2, add=0))
    scopies[1].wait_recv()
    scopies.append(ship(3, 1, 1, 1, add=1))
    zstep(2)

    lw.wait()

    def value_part(rel, part, first):
        cols = pl.ds(pl.multiple_of(same(rel) * R + part * H, H), H)
        wpart = wg[rel, half[part], :]
        a = jnp.dot(x[:, cols], wpart, preferred_element_type=F32)
        b = jnp.dot(xp[rel, :, half[part]], wpart, preferred_element_type=F32)
        if first:
            vown[...] = a
            vsend[...] = b
        else:
            vown[...] += a
            vsend[...] += b

    value_part(0, 0, True)
    value_part(0, 1, False)
    value_part(1, 1, False)
    value_part(2, 0, False)
    zlast()
    pcopies = []
    for a in (0, 1):
        wpart = wg[0, half[a], :]
        pf[a, 1] = jnp.dot(xn[a, 1], wpart, preferred_element_type=F32)
        pcopies.append(remote(pf.at[a, 1], pfr.at[a], fs.at[a], fr.at[a], peer))
        pf[a, 0] = jnp.dot(xn[a, 0], wpart, preferred_element_type=F32)
    qcopies = []
    for a in (0, 1):
        pcopies[a].wait_recv()
        ps[a] = (pf[a, 0] + pfr[a]).astype(BF16)
        qcopies.append(remote(ps.at[a], pr.at[a], qs.at[a], qr.at[a], same(near[a])))

    fx1.wait_recv()
    value_part(3, 1, False)
    fy0.wait_recv()
    value_part(3, 0, False)
    vcopy = remote(vsend, vrecv, vs, vr, peer)

    for a in (0, 1):
        dcopies[3 + a].wait_recv()
        for i in range(H // step):
            cols = pl.ds(i * step, step)
            here = pl.ds(a * H + i * step, step)
            acc[here, :] += dot_tt(xn[a, 0, :, cols], dvn[a, 0]) + dot_tt(
                xn[a, 1, :, cols], dvn[a, 1]
            )
    c2.wait_recv()
    inv = 1.0 / (cnts[4] + cnts[5])[0:1, 0:1]

    vcopy.wait_recv()
    vown[...] += vrecv[...]
    for a in (0, 1):
        qcopies[a].wait_recv()
        vown[...] += pr[a].astype(F32)

    def contexts(kh, _):
        kcols = pl.ds(pl.multiple_of(kh * HEAD_SIZE, HEAD_SIZE), HEAD_SIZE)
        val = vown[:, kcols].astype(BF16)
        for h in range(GROUP):
            cols = pl.ds(pl.multiple_of((kh * GROUP + h) * HEAD_SIZE, HEAD_SIZE), HEAD_SIZE)
            ctx[:, cols] = dot_tt(pt[kh * GROUP + h], val).astype(BF16)
        return 0

    lax.fori_loop(0, kv, contexts, 0)

    for part in (0, 1):
        scopies[2 + part].wait_recv()
        dw_ref[half[part], :] = (acc[half[part], :] + recvbuf[2 + part].astype(F32)) * inv
    zsent()
    for c in [wx1, wy0, fx1, fy0, vcopy, c0, c1, c2] + sends + xcopies + dcopies + scopies + pcopies + qcopies:
        c.wait_send()


def write_kernel(ctx, dw, ctx_hbm, dw_hbm, sems):
    copies = []
    for src, dst in ((ctx, ctx_hbm), (dw, dw_hbm)):
        rows = src.shape[0] // 2
        for part in range(2):
            here = pl.ds(part * rows, rows)
            copies.append(
                pltpu.make_async_copy(src.at[here], dst.at[here], sems.at[len(copies)])
            )
    for c in copies:
        c.start()
    for c in copies:
        c.wait()


def fused(hidden_in, queries, keys, value_weight, context_grad, doc_ids, token_counts):
    T, M = hidden_in.shape
    C = keys.shape[1]
    Q = queries.shape[1]
    R = value_weight.shape[0]
    heads = Q // HEAD_SIZE
    hbm = pl.BlockSpec(memory_space=pltpu.HBM)
    dma = pltpu.SemaphoreType.DMA
    pinned = [
        pltpu.with_memory_space_constraint(a, pltpu.HBM)
        for a in (hidden_in, queries, keys, value_weight, context_grad, doc_ids)
    ]
    results = tuple(
        pl.pallas_call(
            fused_kernel,
            out_shape=(
                jax.ShapeDtypeStruct((T, Q), BF16),
                jax.ShapeDtypeStruct((R, C), F32),
            ),
            in_specs=[hbm] * 6 + [pl.BlockSpec(memory_space=pltpu.SMEM)],
            out_specs=(pl.BlockSpec(memory_space=pltpu.VMEM),) * 2,
            scratch_shapes=[
                pltpu.VMEM((T, M), BF16),
                pltpu.VMEM((4, T, R), BF16),
                pltpu.VMEM((T, Q), BF16),
                pltpu.VMEM((T, C), BF16),
                pltpu.VMEM((T, Q), BF16),
                pltpu.VMEM((4, R, C), BF16),
                pltpu.VMEM((heads, T, T), BF16),
                pltpu.VMEM((T, T), F32),
                pltpu.VMEM((T, C), BF16),
                pltpu.VMEM((T, C), BF16),
                pltpu.VMEM((2, 2, T, C), BF16),
                pltpu.VMEM((2, 2, T, R // 2), BF16),
                pltpu.VMEM((T, C), F32),
                pltpu.VMEM((T, C), F32),
                pltpu.VMEM((T, C), F32),
                pltpu.VMEM((2, 2, T, C), F32),
                pltpu.VMEM((2, T, C), F32),
                pltpu.VMEM((2, T, C), BF16),
                pltpu.VMEM((2, T, C), BF16),
                pltpu.VMEM((4, R // 2, C), BF16),
                pltpu.VMEM((4, R // 2, C), BF16),
                pltpu.VMEM((R, C), F32),
                pltpu.VMEM((6, 8, 128), F32),
                pltpu.VMEM(doc_ids.shape, jnp.int32),
                dma((6,)),
                dma((4,)), dma((4,)),
                dma((4,)), dma((4,)),
                dma((3,)), dma((3,)),
                dma((5,)), dma((5,)),
                dma, dma,
                dma((4,)), dma((4,)),
                dma((4,)), dma((4,)),
                dma((2, 6)), dma((2, T // PIECE)),
                dma((2,)), dma((2,)),
                dma((2,)), dma((2,)),
            ],
            compiler_params=pltpu.CompilerParams(
                collective_id=0, has_side_effects=True, vmem_limit_bytes=48 * 1024 * 1024
            ),
        )(*pinned, token_counts)
    )
    return tuple(
        pl.pallas_call(
            write_kernel,
            out_shape=tuple(jax.ShapeDtypeStruct(a.shape, a.dtype) for a in results),
            in_specs=[pl.BlockSpec(memory_space=pltpu.VMEM)] * 2,
            out_specs=(hbm, hbm),
            scratch_shapes=[dma((4,))],
        )(*(pltpu.with_memory_space_constraint(a, pltpu.VMEM) for a in results))
    )


def solution(mesh):
    in_specs = (
        P("dp", None),
        P("dp", "tensor"),
        P("dp", "tensor"),
        P("dp", "tensor"),
        P("dp", "tensor"),
        P("dp", None),
        P("dp"),
    )
    out_specs = (P("dp", "tensor"), P("dp", "tensor"))
    body = fused if (mesh.shape["dp"], mesh.shape["tensor"]) == (8, 4) else plain
    return jax.shard_map(body, mesh=mesh, in_specs=in_specs, out_specs=out_specs, check_vma=False)
```

```python
import functools
import math

import jax
import jax.numpy as jnp
from jax import lax
from jax.experimental import pallas as pl
from jax.experimental.pallas import tpu as pltpu
from jax.sharding import PartitionSpec as P

QUERY_HEADS = 64
KEY_VALUE_HEADS = 8
HEAD_SIZE = 128
GROUP = QUERY_HEADS // KEY_VALUE_HEADS
PIECE = 64
MESH = pl.DeviceIdType.MESH
F32 = jnp.float32
BF16 = jnp.bfloat16


def plain(hidden_in, queries, keys, value_weight, context_grad, doc_ids, token_counts):
    tok_rows = hidden_in.shape[0]
    kv_cols = keys.shape[1]
    kv_local = kv_cols // HEAD_SIZE
    scale = 1.0 / math.sqrt(HEAD_SIZE)
    whole = lax.all_gather(value_weight, "dp", axis=0, tiled=True)
    value_states = jnp.dot(hidden_in, whole, preferred_element_type=F32).astype(BF16)
    query_four_axes = queries.reshape(tok_rows, kv_local, GROUP, HEAD_SIZE)
    key_three_axes = keys.reshape(tok_rows, kv_local, HEAD_SIZE)
    scores = (
        jnp.einsum("ikgd,jkd->kgij", query_four_axes, key_three_axes, preferred_element_type=F32)
        * scale
    )
    position = jnp.arange(tok_rows, dtype=jnp.int32)
    doc_here = doc_ids[0]
    allowed = (position[None, :] <= position[:, None]) & (doc_here[:, None] == doc_here[None, :])
    scores = jnp.where(allowed, scores, -jnp.inf)
    top = jnp.max(scores, axis=-1, keepdims=True)
    expo = jnp.exp(scores - top)
    probs = (expo / jnp.sum(expo, axis=-1, keepdims=True)).astype(BF16)
    value_three_axes = value_states.reshape(tok_rows, kv_local, HEAD_SIZE)
    ctx = jnp.einsum("kgij,jkd->ikgd", probs, value_three_axes, preferred_element_type=F32)
    context = ctx.astype(BF16).reshape(tok_rows, kv_local * GROUP * HEAD_SIZE)
    count_here = token_counts[0]
    valid = position < count_here
    masked = jnp.where(valid[:, None], context_grad, jnp.zeros_like(context_grad))
    masked = masked.reshape(tok_rows, kv_local, GROUP, HEAD_SIZE)
    value_gradient = jnp.einsum("kgij,ikgd->jkd", probs, masked, preferred_element_type=F32)
    value_gradient = value_gradient.astype(BF16).reshape(tok_rows, kv_cols)
    count_float = count_here.astype(F32)
    factor = count_float / lax.psum(count_float, "dp")
    full_term = (
        jnp.einsum("tr,tc->rc", hidden_in, value_gradient, preferred_element_type=F32) * factor
    )
    grad = lax.psum_scatter(full_term, "dp", scatter_dimension=0, tiled=True)
    return (context, grad)


def dot_tt(a, b):
    return lax.dot_general(a, b, (((0,), (0,)), ((), ())), preferred_element_type=F32)


def fused_kernel(
    x_hbm, q_hbm, k_hbm, w_hbm, g_hbm, doc_hbm, cnt_ref, ctx, dw_ref,
    x, xp, q, k, g, wg, pt, bias, dv, dvp, dvn, xn, vown, vsend, vrecv, pf, pfr, ps, pr,
    sendbuf, recvbuf, acc, cnts, doc_ref,
    lsem, xs, xr, ws, wr, cs, cr, ds, dr, vs, vr, ss, sr, ns, nr, zs, zr, fs, fr, qs, qr,
):
    me = lax.axis_index("dp")
    plane = lax.axis_index("tensor")
    planes = xn.shape[2] // PIECE
    core = lax.rem(me, 2)
    chip = me // 2
    cx = lax.rem(chip, 2)
    cy = chip // 2
    peer = me + 1 - 2 * core
    T, C = k.shape
    R = w_hbm.shape[0]
    H = R // 2
    kv = C // HEAD_SIZE
    scale = 1.0 / math.sqrt(HEAD_SIZE)

    def chip_at(rel):
        ax = 1 - cx if rel % 2 else cx
        ay = 1 - cy if rel // 2 else cy
        return 2 * ay + ax

    def same(rel):
        return 2 * chip_at(rel) + core

    def cross(rel):
        return 2 * chip_at(rel) + 1 - core

    lk = pltpu.make_async_copy(k_hbm, k, lsem.at[0])
    lq = pltpu.make_async_copy(q_hbm, q, lsem.at[1])
    lg = pltpu.make_async_copy(g_hbm, g, lsem.at[2])
    lx = pltpu.make_async_copy(x_hbm, x, lsem.at[3])
    lw = pltpu.make_async_copy(w_hbm, wg.at[0], lsem.at[4])
    ld = pltpu.make_async_copy(doc_hbm, doc_ref, lsem.at[5])
    for c in (ld, lk, lq, lg, lx, lw):
        c.start()

    bar = pltpu.get_barrier_semaphore()
    others = (peer, same(1), same(2), cross(1), cross(2))
    for d in others:
        pl.semaphore_signal(bar, inc=1, device_id={"dp": d}, device_id_type=MESH)

    @pl.when(plane > 0)
    def _():
        pl.semaphore_signal(bar, inc=1, device_id={"tensor": plane - 1}, device_id_type=MESH)

    @pl.when(plane < planes - 1)
    def _():
        pl.semaphore_signal(bar, inc=1, device_id={"tensor": plane + 1}, device_id_type=MESH)

    inner = (plane > 0) & (plane < planes - 1)
    pl.semaphore_wait(bar, len(others) + 1 + inner.astype(jnp.int32))

    def remote(src, dst, s, r, dev):
        c = pltpu.make_async_remote_copy(
            src_ref=src, dst_ref=dst, send_sem=s, recv_sem=r,
            device_id={"dp": dev}, device_id_type=MESH,
        )
        c.start()
        return c

    half = (pl.ds(0, H), pl.ds(H, H))
    near = (1, 2)
    sends = []

    rows = pl.ds(pl.multiple_of(plane * PIECE, PIECE), PIECE)
    for a in (0, 1):
        n = near[a]
        for other in (0, 1):
            dev = cross(n) if other else same(n)
            cols = pl.ds(pl.multiple_of(dev * R + a * H, H), H)
            i = 2 * a + other
            sends.append(
                remote(x_hbm.at[rows, cols], xn.at[a, other, rows, :], ns.at[i], nr.at[i], dev)
            )
    direct = list(sends)

    def own_half(rel, part):
        i = part
        return remote(
            w_hbm.at[half[part]], wg.at[rel, half[part]], ws.at[i], wr.at[i], same(rel)
        )

    def onward(src, part):
        i = 2 + part
        return remote(
            wg.at[src, half[part]], wg.at[3, half[part]], ws.at[i], wr.at[i], same(3 - src)
        )

    wx1, wy0 = own_half(1, 1), own_half(2, 0)
    count = cnt_ref[0].astype(F32)
    cnts[0] = jnp.full(cnts.shape[1:], count, F32)
    c0 = remote(cnts.at[0], cnts.at[1], cs.at[0], cr.at[0], peer)
    xcopies = []
    for i, (rel, part) in enumerate(((3, None), (0, None), (1, 1), (2, 0))):
        first = cross(rel) * R
        if part is None:
            src = x_hbm.at[:, pl.ds(pl.multiple_of(first, R), R)]
            dst = xp.at[rel]
        else:
            src = x_hbm.at[:, pl.ds(pl.multiple_of(first + part * H, H), H)]
            dst = xp.at[rel, :, half[part]]
        xcopies.append(remote(src, dst, xs.at[i], xr.at[i], peer))

    def zcopy(a, piece, to, slot):
        rows = pl.ds(pl.multiple_of(piece * PIECE, PIECE), PIECE)
        return pltpu.make_async_remote_copy(
            src_ref=xn.at[a, :, rows, :], dst_ref=xn.at[a, :, rows, :],
            send_sem=zs.at[a, slot], recv_sem=zr.at[a, piece],
            device_id={"tensor": to}, device_id_type=MESH,
        )

    def zmoves(step):
        down, up = plane + step, plane - step
        return (
            (down, plane - 1, (plane > 0) & (down < planes), 2 * step),
            (up, plane + 1, (plane < planes - 1) & (up >= 0), 2 * step + 1),
        )

    def zwait(a, piece):
        zcopy(a, piece, plane, 0).wait_recv()

    def zstep(step, a):
        for piece, to, has, slot in zmoves(step):
            if step:
                @pl.when((piece >= 0) & (piece < planes))
                def _(piece=piece):
                    zwait(a, piece)

            if step < planes - 1:
                @pl.when(has)
                def _(piece=piece, to=to, slot=slot):
                    zcopy(a, piece, to, slot).start()

    def zsent():
        for step in range(planes - 1):
            for a in (0, 1):
                for piece, to, has, slot in zmoves(step):
                    @pl.when(has)
                    def _(a=a, piece=piece, to=to, slot=slot):
                        zcopy(a, piece, to, slot).wait_send()

    ld.wait()
    docs = jnp.broadcast_to(doc_ref[...].astype(F32), (T, T))
    jj = lax.broadcasted_iota(jnp.int32, (T, T), 0)
    ii = lax.broadcasted_iota(jnp.int32, (T, T), 1)
    allowed = (jj <= ii) & (docs == docs.T)
    bias[...] = jnp.where(allowed, 0.0, -jnp.inf).astype(F32)
    lk.wait()
    lq.wait()
    lg.wait()
    row = lax.broadcasted_iota(jnp.int32, (T, HEAD_SIZE), 0).astype(F32)

    def group(kh, _):
        kcols = pl.ds(pl.multiple_of(kh * HEAD_SIZE, HEAD_SIZE), HEAD_SIZE)
        keyg = k[:, kcols]
        total = jnp.zeros((T, HEAD_SIZE), F32)
        for h in range(GROUP):
            cols = pl.ds(pl.multiple_of((kh * GROUP + h) * HEAD_SIZE, HEAD_SIZE), HEAD_SIZE)
            st = lax.dot_general(
                keyg, q[:, cols], (((1,), (1,)), ((), ())), preferred_element_type=F32
            )
            st = st * scale + bias[...]
            e = jnp.exp(st - jnp.max(st, axis=0, keepdims=True))
            p = (e * (1.0 / jnp.sum(e, axis=0, keepdims=True))).astype(BF16)
            pt[kh * GROUP + h] = p
            gm = jnp.where(row < count, g[:, cols].astype(F32), 0.0).astype(BF16)
            total = total + jnp.dot(p, gm, preferred_element_type=F32)
        dv[:, kcols] = (total * count).astype(BF16)
        return 0

    lax.fori_loop(0, kv, group, 0)
    dcopies = [remote(dv, dvp, ds.at[0], dr.at[0], peer)]
    for a in (0, 1):
        direct[2 * a].wait_recv()
        direct[2 * a + 1].wait_recv()
        zstep(0, a)
    c0.wait_recv()
    cnts[2] = cnts[0] + cnts[1]
    c1 = remote(cnts.at[2], cnts.at[3], cs.at[1], cr.at[1], same(1))
    lx.wait()
    for c in xcopies:
        c.wait_recv()
    dcopies[0].wait_recv()
    step = min(256, H)

    def partial(rel, part, store):
        base = same(rel) * R
        first = part * H

        def body(t, _):
            off = pl.multiple_of(first + t * step, step)
            xa = x[:, pl.ds(pl.multiple_of(base + off, step), step)]
            xb = xp[rel, :, pl.ds(off, step)]
            store(off, dot_tt(xa, dv[...]) + dot_tt(xb, dvp[...]))
            return 0

        lax.fori_loop(0, H // step, body, 0)

    def send_block(slot, first, size, i, to):
        here = pl.ds(first, size)
        return remote(
            sendbuf.at[slot, here], recvbuf.at[slot, here], ss.at[i], sr.at[i], same(to)
        )

    def fill(slot, rel, part, add=None):
        def put(off, val):
            here = pl.ds(off - part * H, step)
            if add is not None:
                val = val + recvbuf[add, here, :].astype(F32)
            sendbuf[slot, here, :] = val.astype(BF16)

        partial(rel, part, put)

    def keep(off, val):
        acc[pl.ds(off, step), :] = val

    def value_part(rel, part, first=False):
        cols = pl.ds(pl.multiple_of(same(rel) * R + part * H, H), H)
        wpart = wg[rel, half[part], :]
        a = jnp.dot(x[:, cols], wpart, preferred_element_type=F32)
        b = jnp.dot(xp[rel, :, half[part]], wpart, preferred_element_type=F32)
        if first:
            vown[...] = a
            vsend[...] = b
        else:
            vown[...] += a
            vsend[...] += b

    scopies = []
    for part in (0, 1):
        fill(part, 3, part)
        scopies.append(send_block(part, 0, H, part, near[part]))
    partial(0, 0, keep)
    zstep(1, 0)
    partial(0, 1, keep)
    lw.wait()
    value_part(0, 0, True)
    value_part(0, 1)
    wx1.wait_recv()
    fx1 = onward(1, 1)
    wy0.wait_recv()
    fy0 = onward(2, 0)
    dcopies.append(remote(dv, dvn.at[0, 0], ds.at[1], dr.at[1], same(1)))
    dcopies.append(remote(dv, dvn.at[1, 0], ds.at[2], dr.at[2], same(2)))
    value_part(1, 1)
    value_part(2, 0)
    zstep(1, 1)
    c1.wait_recv()
    cnts[4] = cnts[2] + cnts[3]
    c2 = remote(cnts.at[4], cnts.at[5], cs.at[2], cr.at[2], same(2))
    zstep(2, 0)
    for part in (0, 1):
        scopies[part].wait_recv()
        fill(2 + part, near[1 - part], part, add=part)
        scopies.append(send_block(2 + part, 0, H // 2, 2 + part, near[1 - part]))
        if part == 0:
            zstep(2, 1)

    def partial_value(a):
        wpart = wg[0, half[a], :]
        pf[a, 1] = jnp.dot(xn[a, 1], wpart, preferred_element_type=F32)
        c = remote(pf.at[a, 1], pfr.at[a], fs.at[a], fr.at[a], peer)
        pf[a, 0] = jnp.dot(xn[a, 0], wpart, preferred_element_type=F32)
        return c

    def return_value(a):
        pcopies[a].wait_recv()
        ps[a] = (pf[a, 0] + pfr[a]).astype(BF16)
        return remote(ps.at[a], pr.at[a], qs.at[a], qr.at[a], same(near[a]))

    zstep(3, 0)
    pcopies = [partial_value(0)]
    fx1.wait_recv()
    value_part(3, 1)
    qcopies = [return_value(0)]
    fy0.wait_recv()
    value_part(3, 0)
    vcopy = remote(vsend, vrecv, vs, vr, peer)
    zstep(3, 1)
    pcopies.append(partial_value(1))
    vcopy.wait_recv()
    vown[...] += vrecv[...]
    qcopies.append(return_value(1))
    for part in (0, 1):
        scopies.append(send_block(2 + part, H // 2, H // 2, 4 + part, near[1 - part]))

    for a in (0, 1):
        dcopies[1 + a].wait_recv()
        dcopies.append(
            remote(dvn.at[a, 0], dvn.at[a, 1], ds.at[3 + a], dr.at[3 + a], peer)
        )
    for a in (0, 1):
        dcopies[3 + a].wait_recv()
        for i in range(H // step):
            cols = pl.ds(i * step, step)
            here = pl.ds(a * H + i * step, step)
            acc[here, :] += dot_tt(xn[a, 0, :, cols], dvn[a, 0]) + dot_tt(
                xn[a, 1, :, cols], dvn[a, 1]
            )
    c2.wait_recv()
    inv = 1.0 / (cnts[4] + cnts[5])[0:1, 0:1]
    for a in (0, 1):
        qcopies[a].wait_recv()
        vown[...] += pr[a].astype(F32)

    def contexts(kh, _):
        kcols = pl.ds(pl.multiple_of(kh * HEAD_SIZE, HEAD_SIZE), HEAD_SIZE)
        val = vown[:, kcols].astype(BF16)
        for h in range(GROUP):
            cols = pl.ds(pl.multiple_of((kh * GROUP + h) * HEAD_SIZE, HEAD_SIZE), HEAD_SIZE)
            ctx[:, cols] = dot_tt(pt[kh * GROUP + h], val).astype(BF16)
        return 0

    lax.fori_loop(0, kv, contexts, 0)

    for i in (0, 1):
        for part in (0, 1):
            scopies[2 + 2 * i + part].wait_recv()
            got = recvbuf[2 + part, pl.ds(i * H // 2, H // 2), :].astype(F32)
            here = pl.ds(part * H + i * H // 2, H // 2)
            dw_ref[here, :] = (acc[here, :] + got) * inv
    zsent()
    for c in [wx1, wy0, fx1, fy0, vcopy, c0, c1, c2] + sends + xcopies + dcopies + scopies + pcopies + qcopies:
        c.wait_send()


def write_kernel(ctx, dw, ctx_hbm, dw_hbm, sems):
    copies = []
    for src, dst in ((ctx, ctx_hbm), (dw, dw_hbm)):
        rows = src.shape[0] // 2
        for part in range(2):
            here = pl.ds(part * rows, rows)
            copies.append(
                pltpu.make_async_copy(src.at[here], dst.at[here], sems.at[len(copies)])
            )
    for c in copies:
        c.start()
    for c in copies:
        c.wait()


def fused(hidden_in, queries, keys, value_weight, context_grad, doc_ids, token_counts):
    T, M = hidden_in.shape
    C = keys.shape[1]
    Q = queries.shape[1]
    R = value_weight.shape[0]
    heads = Q // HEAD_SIZE
    hbm = pl.BlockSpec(memory_space=pltpu.HBM)
    dma = pltpu.SemaphoreType.DMA
    pinned = [
        pltpu.with_memory_space_constraint(a, pltpu.HBM)
        for a in (hidden_in, queries, keys, value_weight, context_grad, doc_ids)
    ]
    results = tuple(
        pl.pallas_call(
            fused_kernel,
            out_shape=(
                jax.ShapeDtypeStruct((T, Q), BF16),
                jax.ShapeDtypeStruct((R, C), F32),
            ),
            in_specs=[hbm] * 6 + [pl.BlockSpec(memory_space=pltpu.SMEM)],
            out_specs=(pl.BlockSpec(memory_space=pltpu.VMEM),) * 2,
            scratch_shapes=[
                pltpu.VMEM((T, M), BF16),
                pltpu.VMEM((4, T, R), BF16),
                pltpu.VMEM((T, Q), BF16),
                pltpu.VMEM((T, C), BF16),
                pltpu.VMEM((T, Q), BF16),
                pltpu.VMEM((4, R, C), BF16),
                pltpu.VMEM((heads, T, T), BF16),
                pltpu.VMEM((T, T), F32),
                pltpu.VMEM((T, C), BF16),
                pltpu.VMEM((T, C), BF16),
                pltpu.VMEM((2, 2, T, C), BF16),
                pltpu.VMEM((2, 2, T, R // 2), BF16),
                pltpu.VMEM((T, C), F32),
                pltpu.VMEM((T, C), F32),
                pltpu.VMEM((T, C), F32),
                pltpu.VMEM((2, 2, T, C), F32),
                pltpu.VMEM((2, T, C), F32),
                pltpu.VMEM((2, T, C), BF16),
                pltpu.VMEM((2, T, C), BF16),
                pltpu.VMEM((4, R // 2, C), BF16),
                pltpu.VMEM((4, R // 2, C), BF16),
                pltpu.VMEM((R, C), F32),
                pltpu.VMEM((6, 8, 128), F32),
                pltpu.VMEM(doc_ids.shape, jnp.int32),
                dma((6,)),
                dma((4,)), dma((4,)),
                dma((4,)), dma((4,)),
                dma((3,)), dma((3,)),
                dma((5,)), dma((5,)),
                dma, dma,
                dma((6,)), dma((6,)),
                dma((4,)), dma((4,)),
                dma((2, 6)), dma((2, T // PIECE)),
                dma((2,)), dma((2,)),
                dma((2,)), dma((2,)),
            ],
            compiler_params=pltpu.CompilerParams(
                collective_id=0, has_side_effects=True, vmem_limit_bytes=48 * 1024 * 1024
            ),
        )(*pinned, token_counts)
    )
    return tuple(
        pl.pallas_call(
            write_kernel,
            out_shape=tuple(jax.ShapeDtypeStruct(a.shape, a.dtype) for a in results),
            in_specs=[pl.BlockSpec(memory_space=pltpu.VMEM)] * 2,
            out_specs=(hbm, hbm),
            scratch_shapes=[dma((4,))],
        )(*(pltpu.with_memory_space_constraint(a, pltpu.VMEM) for a in results))
    )


def solution(mesh):
    in_specs = (
        P("dp", None),
        P("dp", "tensor"),
        P("dp", "tensor"),
        P("dp", "tensor"),
        P("dp", "tensor"),
        P("dp", None),
        P("dp"),
    )
    out_specs = (P("dp", "tensor"), P("dp", "tensor"))
    body = fused if (mesh.shape["dp"], mesh.shape["tensor"]) == (8, 4) else plain
    return jax.shard_map(body, mesh=mesh, in_specs=in_specs, out_specs=out_specs, check_vma=False)
```

```python
import functools
import math

import jax
import jax.numpy as jnp
from jax import lax
from jax.experimental import pallas as pl
from jax.experimental.pallas import tpu as pltpu
from jax.sharding import PartitionSpec as P

QUERY_HEADS = 64
KEY_VALUE_HEADS = 8
HEAD_SIZE = 128
GROUP = QUERY_HEADS // KEY_VALUE_HEADS
SMALL = 64
MESH = pl.DeviceIdType.MESH
F32 = jnp.float32
BF16 = jnp.bfloat16


def plain(hidden_in, queries, keys, value_weight, context_grad, doc_ids, token_counts):
    tok_rows = hidden_in.shape[0]
    kv_cols = keys.shape[1]
    kv_local = kv_cols // HEAD_SIZE
    scale = 1.0 / math.sqrt(HEAD_SIZE)
    whole = lax.all_gather(value_weight, "dp", axis=0, tiled=True)
    value_states = jnp.dot(hidden_in, whole, preferred_element_type=F32).astype(BF16)
    query_four_axes = queries.reshape(tok_rows, kv_local, GROUP, HEAD_SIZE)
    key_three_axes = keys.reshape(tok_rows, kv_local, HEAD_SIZE)
    scores = (
        jnp.einsum("ikgd,jkd->kgij", query_four_axes, key_three_axes, preferred_element_type=F32)
        * scale
    )
    position = jnp.arange(tok_rows, dtype=jnp.int32)
    doc_here = doc_ids[0]
    allowed = (position[None, :] <= position[:, None]) & (doc_here[:, None] == doc_here[None, :])
    scores = jnp.where(allowed, scores, -jnp.inf)
    top = jnp.max(scores, axis=-1, keepdims=True)
    expo = jnp.exp(scores - top)
    probs = (expo / jnp.sum(expo, axis=-1, keepdims=True)).astype(BF16)
    value_three_axes = value_states.reshape(tok_rows, kv_local, HEAD_SIZE)
    ctx = jnp.einsum("kgij,jkd->ikgd", probs, value_three_axes, preferred_element_type=F32)
    context = ctx.astype(BF16).reshape(tok_rows, kv_local * GROUP * HEAD_SIZE)
    count_here = token_counts[0]
    valid = position < count_here
    masked = jnp.where(valid[:, None], context_grad, jnp.zeros_like(context_grad))
    masked = masked.reshape(tok_rows, kv_local, GROUP, HEAD_SIZE)
    value_gradient = jnp.einsum("kgij,ikgd->jkd", probs, masked, preferred_element_type=F32)
    value_gradient = value_gradient.astype(BF16).reshape(tok_rows, kv_cols)
    count_float = count_here.astype(F32)
    factor = count_float / lax.psum(count_float, "dp")
    full_term = (
        jnp.einsum("tr,tc->rc", hidden_in, value_gradient, preferred_element_type=F32) * factor
    )
    grad = lax.psum_scatter(full_term, "dp", scatter_dimension=0, tiled=True)
    return (context, grad)


def dot_tt(a, b):
    return lax.dot_general(a, b, (((0,), (0,)), ((), ())), preferred_element_type=F32)


def fused_kernel(
    x_hbm, q_hbm, k_hbm, w_hbm, g_hbm, doc_hbm, cnt_ref, ctx, dw_ref,
    x, xp, xq, q, k, g, wg, pt, bias, dv, dvp, dvn, xn, vown, vsend, vrecv, pf, pfr, ps, pr,
    sendbuf, recvbuf, acc, cnts, doc_ref,
    lsem, xs, xr, ws, wr, cs, cr, ds, dr, vs, vr, ss, sr, ns, nr, zs, zr, fs, fr, qs, qr, us, ur,
):
    me = lax.axis_index("dp")
    plane = lax.axis_index("tensor")
    planes = zr.shape[1]
    big = xq.shape[1]
    core = lax.rem(me, 2)
    chip = me // 2
    cx = lax.rem(chip, 2)
    cy = chip // 2
    peer = me + 1 - 2 * core
    T, C = k.shape
    R = w_hbm.shape[0]
    H = R // 2
    kv = C // HEAD_SIZE
    scale = 1.0 / math.sqrt(HEAD_SIZE)

    def chip_at(rel):
        ax = 1 - cx if rel % 2 else cx
        ay = 1 - cy if rel // 2 else cy
        return 2 * ay + ax

    def same(rel):
        return 2 * chip_at(rel) + core

    def cross(rel):
        return 2 * chip_at(rel) + 1 - core

    lk = pltpu.make_async_copy(k_hbm, k, lsem.at[0])
    lq = pltpu.make_async_copy(q_hbm, q, lsem.at[1])
    lg = pltpu.make_async_copy(g_hbm, g, lsem.at[2])
    lx = pltpu.make_async_copy(x_hbm, x, lsem.at[3])
    lw = pltpu.make_async_copy(w_hbm, wg.at[0], lsem.at[4])
    ld = pltpu.make_async_copy(doc_hbm, doc_ref, lsem.at[5])
    for c in (ld, lk, lq, lg, lx, lw):
        c.start()

    bar = pltpu.get_barrier_semaphore()
    others = (peer, same(1), same(2))
    for d in others:
        pl.semaphore_signal(bar, inc=1, device_id={"dp": d}, device_id_type=MESH)

    @pl.when(plane > 0)
    def _():
        pl.semaphore_signal(bar, inc=1, device_id={"tensor": plane - 1}, device_id_type=MESH)

    @pl.when(plane < planes - 1)
    def _():
        pl.semaphore_signal(bar, inc=1, device_id={"tensor": plane + 1}, device_id_type=MESH)

    inner = (plane > 0) & (plane < planes - 1)
    pl.semaphore_wait(bar, len(others) + 1 + inner.astype(jnp.int32))

    def remote(src, dst, s, r, dev):
        c = pltpu.make_async_remote_copy(
            src_ref=src, dst_ref=dst, send_sem=s, recv_sem=r,
            device_id={"dp": dev}, device_id_type=MESH,
        )
        c.start()
        return c

    half = (pl.ds(0, H), pl.ds(H, H))
    near = (1, 2)

    def each(piece, act):
        @pl.when(piece == 0)
        def _():
            act(0, SMALL)

        @pl.when(piece > 0)
        def _():
            act(pl.multiple_of(SMALL + (piece - 1) * big, 16), big)

    def owned(block, a, first, size):
        cols = pl.ds(pl.multiple_of(block * R + a * H, H), H)
        return x_hbm.at[pl.ds(first, size), cols]

    def swap(a, first, size):
        return pltpu.make_async_remote_copy(
            src_ref=owned(cross(near[a]), a, first, size), dst_ref=xq.at[a, pl.ds(0, size), :],
            send_sem=us.at[a], recv_sem=ur.at[a],
            device_id={"dp": peer}, device_id_type=MESH,
        )

    def direct(a, j, first, size):
        n = same(near[a])
        src = xq.at[a, pl.ds(0, size), :] if j else owned(n, a, first, size)
        return pltpu.make_async_remote_copy(
            src_ref=src, dst_ref=xn.at[a, j, pl.ds(first, size), :],
            send_sem=ns.at[2 * a + j], recv_sem=nr.at[2 * a + j],
            device_id={"dp": n}, device_id_type=MESH,
        )

    def begin(first, size):
        for a in (0, 1):
            swap(a, first, size).start()
        for a in (0, 1):
            direct(a, 0, first, size).start()
        for a in (0, 1):
            swap(a, first, size).wait_recv()
            direct(a, 1, first, size).start()

    each(plane, begin)

    def own_half(rel, part):
        i = part
        return remote(
            w_hbm.at[half[part]], wg.at[rel, half[part]], ws.at[i], wr.at[i], same(rel)
        )

    def onward(src, part):
        i = 2 + part
        return remote(
            wg.at[src, half[part]], wg.at[3, half[part]], ws.at[i], wr.at[i], same(3 - src)
        )

    wx1, wy0 = own_half(1, 1), own_half(2, 0)
    count = cnt_ref[0].astype(F32)
    cnts[0] = jnp.full(cnts.shape[1:], count, F32)
    c0 = remote(cnts.at[0], cnts.at[1], cs.at[0], cr.at[0], peer)
    xcopies = []
    for i, (rel, part) in enumerate(((3, None), (0, None), (1, 1), (2, 0))):
        first = cross(rel) * R
        if part is None:
            src = x_hbm.at[:, pl.ds(pl.multiple_of(first, R), R)]
            dst = xp.at[rel]
        else:
            src = x_hbm.at[:, pl.ds(pl.multiple_of(first + part * H, H), H)]
            dst = xp.at[rel, :, half[part]]
        xcopies.append(remote(src, dst, xs.at[i], xr.at[i], peer))

    def zcopy(a, j, piece, to, slot, first, size):
        here = xn.at[a, j, pl.ds(first, size), :]
        return pltpu.make_async_remote_copy(
            src_ref=here, dst_ref=here,
            send_sem=zs.at[2 * a + j, slot], recv_sem=zr.at[2 * a + j, piece],
            device_id={"tensor": to}, device_id_type=MESH,
        )

    def zmoves(step):
        down, up = plane + step, plane - step
        return (
            (down, plane - 1, (plane > 0) & (down < planes), 2 * step),
            (up, plane + 1, (plane < planes - 1) & (up >= 0), 2 * step + 1),
        )

    def spread(a):
        def act(first, size):
            for j in (0, 1):
                direct(a, j, first, size).wait_recv()
                for piece, to, has, slot in zmoves(0):
                    @pl.when(has)
                    def _(j=j, piece=piece, to=to, slot=slot):
                        zcopy(a, j, piece, to, slot, first, size).start()

        each(plane, act)

    def zstep(step, a):
        for piece, to, has, slot in zmoves(step):
            def act(first, size, piece=piece, to=to, has=has, slot=slot):
                for j in (0, 1):
                    zcopy(a, j, piece, to, slot, first, size).wait_recv()
                    if step < planes - 1:
                        @pl.when(has)
                        def _(j=j):
                            zcopy(a, j, piece, to, slot, first, size).start()

            @pl.when((piece >= 0) & (piece < planes))
            def _(piece=piece, act=act):
                each(piece, act)

    def xsent():
        def own(first, size):
            for a in (0, 1):
                swap(a, first, size).wait_send()
                for j in (0, 1):
                    direct(a, j, first, size).wait_send()

        each(plane, own)
        for step in range(planes - 1):
            for piece, to, has, slot in zmoves(step):
                def act(first, size, piece=piece, to=to, slot=slot):
                    for a in (0, 1):
                        for j in (0, 1):
                            zcopy(a, j, piece, to, slot, first, size).wait_send()

                @pl.when(has)
                def _(piece=piece, act=act):
                    each(piece, act)

    ld.wait()
    docs = jnp.broadcast_to(doc_ref[...].astype(F32), (T, T))
    jj = lax.broadcasted_iota(jnp.int32, (T, T), 0)
    ii = lax.broadcasted_iota(jnp.int32, (T, T), 1)
    allowed = (jj <= ii) & (docs == docs.T)
    bias[...] = jnp.where(allowed, 0.0, -jnp.inf).astype(F32)
    lk.wait()
    lq.wait()
    lg.wait()
    row = lax.broadcasted_iota(jnp.int32, (T, HEAD_SIZE), 0).astype(F32)

    def group(kh, _):
        kcols = pl.ds(pl.multiple_of(kh * HEAD_SIZE, HEAD_SIZE), HEAD_SIZE)
        keyg = k[:, kcols]
        total = jnp.zeros((T, HEAD_SIZE), F32)
        for h in range(GROUP):
            cols = pl.ds(pl.multiple_of((kh * GROUP + h) * HEAD_SIZE, HEAD_SIZE), HEAD_SIZE)
            st = lax.dot_general(
                keyg, q[:, cols], (((1,), (1,)), ((), ())), preferred_element_type=F32
            )
            st = st * scale + bias[...]
            e = jnp.exp(st - jnp.max(st, axis=0, keepdims=True))
            p = (e * (1.0 / jnp.sum(e, axis=0, keepdims=True))).astype(BF16)
            pt[kh * GROUP + h] = p
            gm = jnp.where(row < count, g[:, cols].astype(F32), 0.0).astype(BF16)
            total = total + jnp.dot(p, gm, preferred_element_type=F32)
        dv[:, kcols] = (total * count).astype(BF16)
        return 0

    lax.fori_loop(0, kv, group, 0)
    dcopies = [remote(dv, dvp, ds.at[0], dr.at[0], peer)]
    for a in (0, 1):
        spread(a)
    c0.wait_recv()
    cnts[2] = cnts[0] + cnts[1]
    c1 = remote(cnts.at[2], cnts.at[3], cs.at[1], cr.at[1], same(1))
    lx.wait()
    for c in xcopies:
        c.wait_recv()
    dcopies[0].wait_recv()
    step = min(256, H)

    def partial(rel, part, store):
        base = same(rel) * R
        first = part * H

        def body(t, _):
            off = pl.multiple_of(first + t * step, step)
            xa = x[:, pl.ds(pl.multiple_of(base + off, step), step)]
            xb = xp[rel, :, pl.ds(off, step)]
            store(off, dot_tt(xa, dv[...]) + dot_tt(xb, dvp[...]))
            return 0

        lax.fori_loop(0, H // step, body, 0)

    def send_block(slot, first, size, i, to):
        here = pl.ds(first, size)
        return remote(
            sendbuf.at[slot, here], recvbuf.at[slot, here], ss.at[i], sr.at[i], same(to)
        )

    def fill(slot, rel, part, add=None):
        def put(off, val):
            here = pl.ds(off - part * H, step)
            if add is not None:
                val = val + recvbuf[add, here, :].astype(F32)
            sendbuf[slot, here, :] = val.astype(BF16)

        partial(rel, part, put)

    def keep(off, val):
        acc[pl.ds(off, step), :] = val

    def value_part(rel, part, first=False):
        cols = pl.ds(pl.multiple_of(same(rel) * R + part * H, H), H)
        wpart = wg[rel, half[part], :]
        a = jnp.dot(x[:, cols], wpart, preferred_element_type=F32)
        b = jnp.dot(xp[rel, :, half[part]], wpart, preferred_element_type=F32)
        if first:
            vown[...] = a
            vsend[...] = b
        else:
            vown[...] += a
            vsend[...] += b

    scopies = []
    for part in (0, 1):
        fill(part, 3, part)
        scopies.append(send_block(part, 0, H, part, near[part]))
    partial(0, 0, keep)
    zstep(1, 0)
    partial(0, 1, keep)
    lw.wait()
    value_part(0, 0, True)
    value_part(0, 1)
    wx1.wait_recv()
    fx1 = onward(1, 1)
    wy0.wait_recv()
    fy0 = onward(2, 0)
    dcopies.append(remote(dv, dvn.at[0, 0], ds.at[1], dr.at[1], same(1)))
    dcopies.append(remote(dv, dvn.at[1, 0], ds.at[2], dr.at[2], same(2)))
    value_part(1, 1)
    value_part(2, 0)
    zstep(1, 1)
    c1.wait_recv()
    cnts[4] = cnts[2] + cnts[3]
    c2 = remote(cnts.at[4], cnts.at[5], cs.at[2], cr.at[2], same(2))
    zstep(2, 0)
    first = H * 256 // 512
    for part in (0, 1):
        scopies[part].wait_recv()
        fill(2 + part, near[1 - part], part, add=part)
        if part == 0:
            zstep(2, 1)

    late = jnp.where(plane < planes // 2, T - big, 0)
    early = jnp.where(plane < planes // 2, 0, big)
    goes = (
        pl.ds(pl.multiple_of(early, 16), T - big),
        pl.ds(pl.multiple_of(late, 16), big),
    )

    def partial_value(a, go):
        rows = goes[go]
        i = 2 * go + a
        wpart = wg[0, half[a], :]
        pf[a, 1, rows, :] = jnp.dot(xn[a, 1, rows, :], wpart, preferred_element_type=F32)
        c = remote(pf.at[a, 1, rows, :], pfr.at[a, rows, :], fs.at[i], fr.at[i], peer)
        pf[a, 0, rows, :] = jnp.dot(xn[a, 0, rows, :], wpart, preferred_element_type=F32)
        return c

    def return_value(a, go):
        rows = goes[go]
        i = 2 * go + a
        pcopies[i].wait_recv()
        ps[a, rows, :] = (pf[a, 0, rows, :] + pfr[a, rows, :]).astype(BF16)
        return remote(
            ps.at[a, rows, :], pr.at[a, rows, :], qs.at[i], qr.at[i], same(near[a])
        )

    pcopies = [partial_value(0, 0), partial_value(1, 0)]
    qcopies = [return_value(0, 0), return_value(1, 0)]
    for part in (0, 1):
        scopies.append(send_block(2 + part, 0, first, 2 + part, near[1 - part]))
    fx1.wait_recv()
    value_part(3, 1)
    fy0.wait_recv()
    value_part(3, 0)
    vcopy = remote(vsend, vrecv, vs, vr, peer)
    zstep(3, 0)
    pcopies.append(partial_value(0, 1))
    zstep(3, 1)
    pcopies.append(partial_value(1, 1))
    for a in (0, 1):
        dcopies[1 + a].wait_recv()
        dcopies.append(
            remote(dvn.at[a, 0], dvn.at[a, 1], ds.at[3 + a], dr.at[3 + a], peer)
        )
    qcopies += [return_value(0, 1), return_value(1, 1)]
    for part in (0, 1):
        scopies.append(send_block(2 + part, first, H - first, 4 + part, near[1 - part]))
    vcopy.wait_recv()
    vown[...] += vrecv[...]
    for a in (0, 1):
        dcopies[3 + a].wait_recv()
        for i in range(H // step):
            cols = pl.ds(i * step, step)
            here = pl.ds(a * H + i * step, step)
            acc[here, :] += dot_tt(xn[a, 0, :, cols], dvn[a, 0]) + dot_tt(
                xn[a, 1, :, cols], dvn[a, 1]
            )
    c2.wait_recv()
    inv = 1.0 / (cnts[4] + cnts[5])[0:1, 0:1]
    def contexts(first, count):
        rows = pl.ds(first, count)

        def body(kh, _):
            kcols = pl.ds(pl.multiple_of(kh * HEAD_SIZE, HEAD_SIZE), HEAD_SIZE)
            val = vown[:, kcols].astype(BF16)
            for h in range(GROUP):
                head = kh * GROUP + h
                cols = pl.ds(pl.multiple_of(head * HEAD_SIZE, HEAD_SIZE), HEAD_SIZE)
                ctx[rows, cols] = dot_tt(pt[head, :, rows], val).astype(BF16)
            return 0

        lax.fori_loop(0, kv, body, 0)

    def add_values(go):
        for a in (0, 1):
            qcopies[2 * go + a].wait_recv()
            vown[goes[go], :] += pr[a, goes[go], :].astype(F32)

    add_values(0)

    @pl.when(plane < planes // 2)
    def _():
        contexts(0, T // 2)

    add_values(1)

    @pl.when(plane >= planes // 2)
    def _():
        contexts(0, T // 2)

    contexts(T // 2, T // 2)

    for i in (0, 1):
        for part in (0, 1):
            scopies[2 + 2 * i + part].wait_recv()
            size = H - first if i else first
            got = recvbuf[2 + part, pl.ds(i * first, size), :].astype(F32)
            here = pl.ds(part * H + i * first, size)
            dw_ref[here, :] = (acc[here, :] + got) * inv
    xsent()
    for c in [wx1, wy0, fx1, fy0, vcopy, c0, c1, c2] + xcopies + dcopies + scopies + pcopies + qcopies:
        c.wait_send()


def write_kernel(ctx, dw, ctx_hbm, dw_hbm, sems):
    copies = []
    for src, dst in ((ctx, ctx_hbm), (dw, dw_hbm)):
        rows = src.shape[0] // 2
        for part in range(2):
            here = pl.ds(part * rows, rows)
            copies.append(
                pltpu.make_async_copy(src.at[here], dst.at[here], sems.at[len(copies)])
            )
    for c in copies:
        c.start()
    for c in copies:
        c.wait()


def fused(planes, hidden_in, queries, keys, value_weight, context_grad, doc_ids, token_counts):
    T, M = hidden_in.shape
    C = keys.shape[1]
    Q = queries.shape[1]
    R = value_weight.shape[0]
    heads = Q // HEAD_SIZE
    hbm = pl.BlockSpec(memory_space=pltpu.HBM)
    dma = pltpu.SemaphoreType.DMA
    pinned = [
        pltpu.with_memory_space_constraint(a, pltpu.HBM)
        for a in (hidden_in, queries, keys, value_weight, context_grad, doc_ids)
    ]
    results = tuple(
        pl.pallas_call(
            fused_kernel,
            out_shape=(
                jax.ShapeDtypeStruct((T, Q), BF16),
                jax.ShapeDtypeStruct((R, C), F32),
            ),
            in_specs=[hbm] * 6 + [pl.BlockSpec(memory_space=pltpu.SMEM)],
            out_specs=(pl.BlockSpec(memory_space=pltpu.VMEM),) * 2,
            scratch_shapes=[
                pltpu.VMEM((T, M), BF16),
                pltpu.VMEM((4, T, R), BF16),
                pltpu.VMEM((2, (T - SMALL) // (planes - 1), R // 2), BF16),
                pltpu.VMEM((T, Q), BF16),
                pltpu.VMEM((T, C), BF16),
                pltpu.VMEM((T, Q), BF16),
                pltpu.VMEM((4, R, C), BF16),
                pltpu.VMEM((heads, T, T), BF16),
                pltpu.VMEM((T, T), F32),
                pltpu.VMEM((T, C), BF16),
                pltpu.VMEM((T, C), BF16),
                pltpu.VMEM((2, 2, T, C), BF16),
                pltpu.VMEM((2, 2, T, R // 2), BF16),
                pltpu.VMEM((T, C), F32),
                pltpu.VMEM((T, C), F32),
                pltpu.VMEM((T, C), F32),
                pltpu.VMEM((2, 2, T, C), F32),
                pltpu.VMEM((2, T, C), F32),
                pltpu.VMEM((2, T, C), BF16),
                pltpu.VMEM((2, T, C), BF16),
                pltpu.VMEM((4, R // 2, C), BF16),
                pltpu.VMEM((4, R // 2, C), BF16),
                pltpu.VMEM((R, C), F32),
                pltpu.VMEM((6, 8, 128), F32),
                pltpu.VMEM(doc_ids.shape, jnp.int32),
                dma((6,)),
                dma((4,)), dma((4,)),
                dma((4,)), dma((4,)),
                dma((3,)), dma((3,)),
                dma((5,)), dma((5,)),
                dma, dma,
                dma((6,)), dma((6,)),
                dma((4,)), dma((4,)),
                dma((4, 2 * (planes - 1))), dma((4, planes)),
                dma((4,)), dma((4,)),
                dma((4,)), dma((4,)),
                dma((2,)), dma((2,)),
            ],
            compiler_params=pltpu.CompilerParams(
                collective_id=0, has_side_effects=True, vmem_limit_bytes=48 * 1024 * 1024
            ),
        )(*pinned, token_counts)
    )
    return tuple(
        pl.pallas_call(
            write_kernel,
            out_shape=tuple(jax.ShapeDtypeStruct(a.shape, a.dtype) for a in results),
            in_specs=[pl.BlockSpec(memory_space=pltpu.VMEM)] * 2,
            out_specs=(hbm, hbm),
            scratch_shapes=[dma((4,))],
        )(*(pltpu.with_memory_space_constraint(a, pltpu.VMEM) for a in results))
    )


def solution(mesh):
    in_specs = (
        P("dp", None),
        P("dp", "tensor"),
        P("dp", "tensor"),
        P("dp", "tensor"),
        P("dp", "tensor"),
        P("dp", None),
        P("dp"),
    )
    out_specs = (P("dp", "tensor"), P("dp", "tensor"))
    planes = mesh.shape["tensor"]
    small = (mesh.shape["dp"], planes) == (8, 4)
    body = functools.partial(fused, planes) if small else plain
    return jax.shard_map(body, mesh=mesh, in_specs=in_specs, out_specs=out_specs, check_vma=False)
```

```python
import functools
import math

import jax
import jax.numpy as jnp
from jax import lax
from jax.experimental import pallas as pl
from jax.experimental.pallas import tpu as pltpu
from jax.sharding import PartitionSpec as P

QUERY_HEADS = 64
KEY_VALUE_HEADS = 8
HEAD_SIZE = 128
GROUP = QUERY_HEADS // KEY_VALUE_HEADS
PIECE = 64
MESH = pl.DeviceIdType.MESH
F32 = jnp.float32
BF16 = jnp.bfloat16


def plain(hidden_in, queries, keys, value_weight, context_grad, doc_ids, token_counts):
    tok_rows = hidden_in.shape[0]
    kv_cols = keys.shape[1]
    kv_local = kv_cols // HEAD_SIZE
    scale = 1.0 / math.sqrt(HEAD_SIZE)
    whole = lax.all_gather(value_weight, "dp", axis=0, tiled=True)
    value_states = jnp.dot(hidden_in, whole, preferred_element_type=F32).astype(BF16)
    query_four_axes = queries.reshape(tok_rows, kv_local, GROUP, HEAD_SIZE)
    key_three_axes = keys.reshape(tok_rows, kv_local, HEAD_SIZE)
    scores = (
        jnp.einsum("ikgd,jkd->kgij", query_four_axes, key_three_axes, preferred_element_type=F32)
        * scale
    )
    position = jnp.arange(tok_rows, dtype=jnp.int32)
    doc_here = doc_ids[0]
    allowed = (position[None, :] <= position[:, None]) & (doc_here[:, None] == doc_here[None, :])
    scores = jnp.where(allowed, scores, -jnp.inf)
    top = jnp.max(scores, axis=-1, keepdims=True)
    expo = jnp.exp(scores - top)
    probs = (expo / jnp.sum(expo, axis=-1, keepdims=True)).astype(BF16)
    value_three_axes = value_states.reshape(tok_rows, kv_local, HEAD_SIZE)
    ctx = jnp.einsum("kgij,jkd->ikgd", probs, value_three_axes, preferred_element_type=F32)
    context = ctx.astype(BF16).reshape(tok_rows, kv_local * GROUP * HEAD_SIZE)
    count_here = token_counts[0]
    valid = position < count_here
    masked = jnp.where(valid[:, None], context_grad, jnp.zeros_like(context_grad))
    masked = masked.reshape(tok_rows, kv_local, GROUP, HEAD_SIZE)
    value_gradient = jnp.einsum("kgij,ikgd->jkd", probs, masked, preferred_element_type=F32)
    value_gradient = value_gradient.astype(BF16).reshape(tok_rows, kv_cols)
    count_float = count_here.astype(F32)
    factor = count_float / lax.psum(count_float, "dp")
    full_term = (
        jnp.einsum("tr,tc->rc", hidden_in, value_gradient, preferred_element_type=F32) * factor
    )
    grad = lax.psum_scatter(full_term, "dp", scatter_dimension=0, tiled=True)
    return (context, grad)


def dot_tt(a, b):
    return lax.dot_general(a, b, (((0,), (0,)), ((), ())), preferred_element_type=F32)


def fused_kernel(
    x_hbm, q_hbm, k_hbm, w_hbm, g_hbm, doc_hbm, cnt_ref, ctx, dw_ref,
    x, xp, xf, xq, q, k, g, wg, pt, bias, dv, dvp, dvn, xn, vown, vsend, vrecv, pf, pfr, ps, pr,
    sendbuf, recvbuf, acc, cnts, doc_ref,
    lsem, xs, xr, ws, wr, cs, cr, ds, dr, vs, vr, ss, sr, ns, nr, zs, zr, fs, fr, qs, qr, us, ur,
):
    me = lax.axis_index("dp")
    plane = lax.axis_index("tensor")
    planes = zr.shape[1]
    big = xq.shape[1]
    core = lax.rem(me, 2)
    chip = me // 2
    cx = lax.rem(chip, 2)
    cy = chip // 2
    peer = me + 1 - 2 * core
    T, C = k.shape
    R = w_hbm.shape[0]
    H = R // 2
    kv = C // HEAD_SIZE
    scale = 1.0 / math.sqrt(HEAD_SIZE)

    def chip_at(rel):
        ax = 1 - cx if rel % 2 else cx
        ay = 1 - cy if rel // 2 else cy
        return 2 * ay + ax

    def same(rel):
        return 2 * chip_at(rel) + core

    def cross(rel):
        return 2 * chip_at(rel) + 1 - core

    lk = pltpu.make_async_copy(k_hbm, k, lsem.at[0])
    lq = pltpu.make_async_copy(q_hbm, q, lsem.at[1])
    lg = pltpu.make_async_copy(g_hbm, g, lsem.at[2])
    lx = pltpu.make_async_copy(x_hbm, x, lsem.at[3])
    lw = pltpu.make_async_copy(w_hbm, wg.at[0], lsem.at[4])
    ld = pltpu.make_async_copy(doc_hbm, doc_ref, lsem.at[5])
    def each(piece, act):
        act(pl.multiple_of(piece * PIECE, 16), PIECE)

    near = (1, 2)
    first_row = pl.multiple_of(plane * PIECE, 16)
    fetched = []
    for a, n in enumerate(near):
        for j, block in enumerate((same(n), cross(n))):
            cols = pl.ds(pl.multiple_of(block * R + a * H, H), H)
            fetched.append(
                pltpu.make_async_copy(
                    x_hbm.at[pl.ds(first_row, PIECE), cols], xf.at[a, j], lsem.at[6 + 2 * a + j]
                )
            )
    for c in fetched + [lw, ld, lk, lq, lg, lx]:
        c.start()

    bar = pltpu.get_barrier_semaphore()
    others = (peer, same(1), same(2))
    for d in others:
        pl.semaphore_signal(bar, inc=1, device_id={"dp": d}, device_id_type=MESH)

    @pl.when(plane > 0)
    def _():
        pl.semaphore_signal(bar, inc=1, device_id={"tensor": plane - 1}, device_id_type=MESH)

    @pl.when(plane < planes - 1)
    def _():
        pl.semaphore_signal(bar, inc=1, device_id={"tensor": plane + 1}, device_id_type=MESH)

    inner = (plane > 0) & (plane < planes - 1)
    pl.semaphore_wait(bar, len(others) + 1 + inner.astype(jnp.int32))

    def remote(src, dst, s, r, dev):
        c = pltpu.make_async_remote_copy(
            src_ref=src, dst_ref=dst, send_sem=s, recv_sem=r,
            device_id={"dp": dev}, device_id_type=MESH,
        )
        c.start()
        return c

    half = (pl.ds(0, H), pl.ds(H, H))

    for c in fetched:
        c.wait()
    swaps = [remote(xf.at[a, 1], xq.at[a], us.at[a], ur.at[a], peer) for a in (0, 1)]
    rows = pl.ds(first_row, PIECE)

    def direct(a, j):
        return remote(
            xq.at[a] if j else xf.at[a, 0], xn.at[a, j, rows, :],
            ns.at[2 * a + j], nr.at[2 * a + j], same(near[a]),
        )

    directs = [direct(a, 0) for a in (0, 1)]
    for a in (0, 1):
        swaps[a].wait_recv()
        directs.append(direct(a, 1))
    lw.wait()

    def own_half(rel, part):
        i = part
        return remote(
            wg.at[0, half[part]], wg.at[rel, half[part]], ws.at[i], wr.at[i], same(rel)
        )

    def onward(src, part):
        i = 2 + part
        return remote(
            wg.at[src, half[part]], wg.at[3, half[part]], ws.at[i], wr.at[i], same(3 - src)
        )

    wx1, wy0 = own_half(1, 1), own_half(2, 0)
    count = cnt_ref[0].astype(F32)
    cnts[0] = jnp.full(cnts.shape[1:], count, F32)
    c0 = remote(cnts.at[0], cnts.at[1], cs.at[0], cr.at[0], peer)
    xcopies = []
    for i, (rel, part) in enumerate(((3, None), (0, None), (1, 1), (2, 0))):
        first = cross(rel) * R
        if part is None:
            src = x_hbm.at[:, pl.ds(pl.multiple_of(first, R), R)]
            dst = xp.at[rel]
        else:
            src = x_hbm.at[:, pl.ds(pl.multiple_of(first + part * H, H), H)]
            dst = xp.at[rel, :, half[part]]
        xcopies.append(remote(src, dst, xs.at[i], xr.at[i], peer))

    def zcopy(a, j, piece, to, slot, first, size):
        here = xn.at[a, j, pl.ds(first, size), :]
        return pltpu.make_async_remote_copy(
            src_ref=here, dst_ref=here,
            send_sem=zs.at[2 * a + j, slot], recv_sem=zr.at[2 * a + j, piece],
            device_id={"tensor": to}, device_id_type=MESH,
        )

    def zmoves(step):
        down, up = plane + step, plane - step
        return (
            (down, plane - 1, (plane > 0) & (down < planes), 2 * step),
            (up, plane + 1, (plane < planes - 1) & (up >= 0), 2 * step + 1),
        )

    def spread(a):
        def act(first, size):
            for j in (0, 1):
                directs[2 * j + a].wait_recv()
                for piece, to, has, slot in zmoves(0):
                    @pl.when(has)
                    def _(j=j, piece=piece, to=to, slot=slot):
                        zcopy(a, j, piece, to, slot, first, size).start()

        each(plane, act)

    def zstep(step, a):
        for piece, to, has, slot in zmoves(step):
            def act(first, size, piece=piece, to=to, has=has, slot=slot):
                for j in (0, 1):
                    zcopy(a, j, piece, to, slot, first, size).wait_recv()
                    if step < planes - 1:
                        @pl.when(has)
                        def _(j=j):
                            zcopy(a, j, piece, to, slot, first, size).start()

            @pl.when((piece >= 0) & (piece < planes))
            def _(piece=piece, act=act):
                each(piece, act)

    def xsent():
        for step in range(planes - 1):
            for piece, to, has, slot in zmoves(step):
                def act(first, size, piece=piece, to=to, slot=slot):
                    for a in (0, 1):
                        for j in (0, 1):
                            zcopy(a, j, piece, to, slot, first, size).wait_send()

                @pl.when(has)
                def _(piece=piece, act=act):
                    each(piece, act)

    ld.wait()
    docs = jnp.broadcast_to(doc_ref[...].astype(F32), (T, T))
    jj = lax.broadcasted_iota(jnp.int32, (T, T), 0)
    ii = lax.broadcasted_iota(jnp.int32, (T, T), 1)
    allowed = (jj <= ii) & (docs == docs.T)
    bias[...] = jnp.where(allowed, 0.0, -jnp.inf).astype(F32)
    lk.wait()
    lq.wait()
    lg.wait()
    row = lax.broadcasted_iota(jnp.int32, (T, HEAD_SIZE), 0).astype(F32)

    def group(kh, _):
        kcols = pl.ds(pl.multiple_of(kh * HEAD_SIZE, HEAD_SIZE), HEAD_SIZE)
        keyg = k[:, kcols]
        total = jnp.zeros((T, HEAD_SIZE), F32)
        for h in range(GROUP):
            cols = pl.ds(pl.multiple_of((kh * GROUP + h) * HEAD_SIZE, HEAD_SIZE), HEAD_SIZE)
            st = lax.dot_general(
                keyg, q[:, cols], (((1,), (1,)), ((), ())), preferred_element_type=F32
            )
            st = st * scale + bias[...]
            e = jnp.exp(st - jnp.max(st, axis=0, keepdims=True))
            p = (e * (1.0 / jnp.sum(e, axis=0, keepdims=True))).astype(BF16)
            pt[kh * GROUP + h] = p
            gm = jnp.where(row < count, g[:, cols].astype(F32), 0.0).astype(BF16)
            total = total + jnp.dot(p, gm, preferred_element_type=F32)
        dv[:, kcols] = (total * count).astype(BF16)
        return 0

    lax.fori_loop(0, kv, group, 0)
    dcopies = [remote(dv, dvp, ds.at[0], dr.at[0], peer)]
    for a in (0, 1):
        spread(a)
    c0.wait_recv()
    cnts[2] = cnts[0] + cnts[1]
    c1 = remote(cnts.at[2], cnts.at[3], cs.at[1], cr.at[1], same(1))
    lx.wait()
    for c in xcopies:
        c.wait_recv()
    dcopies[0].wait_recv()
    step = min(256, H)

    def partial(rel, part, store):
        base = same(rel) * R
        first = part * H

        def body(t, _):
            off = pl.multiple_of(first + t * step, step)
            xa = x[:, pl.ds(pl.multiple_of(base + off, step), step)]
            xb = xp[rel, :, pl.ds(off, step)]
            store(off, dot_tt(xa, dv[...]) + dot_tt(xb, dvp[...]))
            return 0

        lax.fori_loop(0, H // step, body, 0)

    def send_block(slot, first, size, i, to):
        here = pl.ds(first, size)
        return remote(
            sendbuf.at[slot, here], recvbuf.at[slot, here], ss.at[i], sr.at[i], same(to)
        )

    def fill(slot, rel, part, add=None):
        def put(off, val):
            here = pl.ds(off - part * H, step)
            if add is not None:
                val = val + recvbuf[add, here, :].astype(F32)
            sendbuf[slot, here, :] = val.astype(BF16)

        partial(rel, part, put)

    def keep(off, val):
        acc[pl.ds(off, step), :] = val

    def value_part(rel, part, first=False):
        cols = pl.ds(pl.multiple_of(same(rel) * R + part * H, H), H)
        wpart = wg[rel, half[part], :]
        a = jnp.dot(x[:, cols], wpart, preferred_element_type=F32)
        b = jnp.dot(xp[rel, :, half[part]], wpart, preferred_element_type=F32)
        if first:
            vown[...] = a
            vsend[...] = b
        else:
            vown[...] += a
            vsend[...] += b

    scopies = []
    for part in (0, 1):
        fill(part, 3, part)
        scopies.append(send_block(part, 0, H, part, near[part]))
    partial(0, 0, keep)
    zstep(1, 0)
    partial(0, 1, keep)
    value_part(0, 0, True)
    value_part(0, 1)
    wx1.wait_recv()
    fx1 = onward(1, 1)
    wy0.wait_recv()
    fy0 = onward(2, 0)
    dcopies.append(remote(dv, dvn.at[0, 0], ds.at[1], dr.at[1], same(1)))
    dcopies.append(remote(dv, dvn.at[1, 0], ds.at[2], dr.at[2], same(2)))
    value_part(1, 1)
    value_part(2, 0)
    zstep(1, 1)
    c1.wait_recv()
    cnts[4] = cnts[2] + cnts[3]
    c2 = remote(cnts.at[4], cnts.at[5], cs.at[2], cr.at[2], same(2))
    zstep(2, 0)
    first = H * 256 // 512
    for part in (0, 1):
        scopies[part].wait_recv()
        fill(2 + part, near[1 - part], part, add=part)
        if part == 0:
            zstep(2, 1)

    late = jnp.where(plane < planes // 2, T - big, 0)
    early = jnp.where(plane < planes // 2, 0, big)
    goes = (
        pl.ds(pl.multiple_of(early, 16), T - big),
        pl.ds(pl.multiple_of(late, 16), big),
    )

    def partial_value(a, go):
        rows = goes[go]
        i = 2 * go + a
        wpart = wg[0, half[a], :]
        pf[a, 1, rows, :] = jnp.dot(xn[a, 1, rows, :], wpart, preferred_element_type=F32)
        c = remote(pf.at[a, 1, rows, :], pfr.at[a, rows, :], fs.at[i], fr.at[i], peer)
        pf[a, 0, rows, :] = jnp.dot(xn[a, 0, rows, :], wpart, preferred_element_type=F32)
        return c

    def return_value(a, go):
        rows = goes[go]
        i = 2 * go + a
        pcopies[i].wait_recv()
        ps[a, rows, :] = (pf[a, 0, rows, :] + pfr[a, rows, :]).astype(BF16)
        return remote(
            ps.at[a, rows, :], pr.at[a, rows, :], qs.at[i], qr.at[i], same(near[a])
        )

    pcopies = [partial_value(0, 0), partial_value(1, 0)]
    qcopies = [return_value(0, 0), return_value(1, 0)]
    for part in (0, 1):
        scopies.append(send_block(2 + part, 0, first, 2 + part, near[1 - part]))
    fx1.wait_recv()
    value_part(3, 1)
    fy0.wait_recv()
    value_part(3, 0)
    vcopy = remote(vsend, vrecv, vs, vr, peer)
    zstep(3, 0)
    pcopies.append(partial_value(0, 1))
    zstep(3, 1)
    pcopies.append(partial_value(1, 1))
    for a in (0, 1):
        dcopies[1 + a].wait_recv()
        dcopies.append(
            remote(dvn.at[a, 0], dvn.at[a, 1], ds.at[3 + a], dr.at[3 + a], peer)
        )
    qcopies += [return_value(0, 1), return_value(1, 1)]
    for part in (0, 1):
        scopies.append(send_block(2 + part, first, H - first, 4 + part, near[1 - part]))
    vcopy.wait_recv()
    vown[...] += vrecv[...]
    for a in (0, 1):
        dcopies[3 + a].wait_recv()
        for i in range(H // step):
            cols = pl.ds(i * step, step)
            here = pl.ds(a * H + i * step, step)
            acc[here, :] += dot_tt(xn[a, 0, :, cols], dvn[a, 0]) + dot_tt(
                xn[a, 1, :, cols], dvn[a, 1]
            )
    c2.wait_recv()
    inv = 1.0 / (cnts[4] + cnts[5])[0:1, 0:1]
    def contexts(first, count):
        rows = pl.ds(first, count)

        def body(kh, _):
            kcols = pl.ds(pl.multiple_of(kh * HEAD_SIZE, HEAD_SIZE), HEAD_SIZE)
            val = vown[:, kcols].astype(BF16)
            for h in range(GROUP):
                head = kh * GROUP + h
                cols = pl.ds(pl.multiple_of(head * HEAD_SIZE, HEAD_SIZE), HEAD_SIZE)
                ctx[rows, cols] = dot_tt(pt[head, :, rows], val).astype(BF16)
            return 0

        lax.fori_loop(0, kv, body, 0)

    def add_values(go):
        for a in (0, 1):
            qcopies[2 * go + a].wait_recv()
            vown[goes[go], :] += pr[a, goes[go], :].astype(F32)

    add_values(0)

    @pl.when(plane < planes // 2)
    def _():
        contexts(0, T // 2)

    add_values(1)

    @pl.when(plane >= planes // 2)
    def _():
        contexts(0, T // 2)

    contexts(T // 2, T // 2)

    for i in (0, 1):
        for part in (0, 1):
            scopies[2 + 2 * i + part].wait_recv()
            size = H - first if i else first
            got = recvbuf[2 + part, pl.ds(i * first, size), :].astype(F32)
            here = pl.ds(part * H + i * first, size)
            dw_ref[here, :] = (acc[here, :] + got) * inv
    xsent()
    for c in [wx1, wy0, fx1, fy0, vcopy, c0, c1, c2] + swaps + directs + xcopies + dcopies + scopies + pcopies + qcopies:
        c.wait_send()


def write_kernel(ctx, dw, ctx_hbm, dw_hbm, sems):
    copies = []
    for src, dst in ((ctx, ctx_hbm), (dw, dw_hbm)):
        rows = src.shape[0] // 2
        for part in range(2):
            here = pl.ds(part * rows, rows)
            copies.append(
                pltpu.make_async_copy(src.at[here], dst.at[here], sems.at[len(copies)])
            )
    for c in copies:
        c.start()
    for c in copies:
        c.wait()


def fused(planes, hidden_in, queries, keys, value_weight, context_grad, doc_ids, token_counts):
    T, M = hidden_in.shape
    C = keys.shape[1]
    Q = queries.shape[1]
    R = value_weight.shape[0]
    heads = Q // HEAD_SIZE
    hbm = pl.BlockSpec(memory_space=pltpu.HBM)
    dma = pltpu.SemaphoreType.DMA
    pinned = [
        pltpu.with_memory_space_constraint(a, pltpu.HBM)
        for a in (hidden_in, queries, keys, value_weight, context_grad, doc_ids)
    ]
    results = tuple(
        pl.pallas_call(
            fused_kernel,
            out_shape=(
                jax.ShapeDtypeStruct((T, Q), BF16),
                jax.ShapeDtypeStruct((R, C), F32),
            ),
            in_specs=[hbm] * 6 + [pl.BlockSpec(memory_space=pltpu.SMEM)],
            out_specs=(pl.BlockSpec(memory_space=pltpu.VMEM),) * 2,
            scratch_shapes=[
                pltpu.VMEM((T, M), BF16),
                pltpu.VMEM((4, T, R), BF16),
                pltpu.VMEM((2, 2, PIECE, R // 2), BF16),
                pltpu.VMEM((2, PIECE, R // 2), BF16),
                pltpu.VMEM((T, Q), BF16),
                pltpu.VMEM((T, C), BF16),
                pltpu.VMEM((T, Q), BF16),
                pltpu.VMEM((4, R, C), BF16),
                pltpu.VMEM((heads, T, T), BF16),
                pltpu.VMEM((T, T), F32),
                pltpu.VMEM((T, C), BF16),
                pltpu.VMEM((T, C), BF16),
                pltpu.VMEM((2, 2, T, C), BF16),
                pltpu.VMEM((2, 2, T, R // 2), BF16),
                pltpu.VMEM((T, C), F32),
                pltpu.VMEM((T, C), F32),
                pltpu.VMEM((T, C), F32),
                pltpu.VMEM((2, 2, T, C), F32),
                pltpu.VMEM((2, T, C), F32),
                pltpu.VMEM((2, T, C), BF16),
                pltpu.VMEM((2, T, C), BF16),
                pltpu.VMEM((4, R // 2, C), BF16),
                pltpu.VMEM((4, R // 2, C), BF16),
                pltpu.VMEM((R, C), F32),
                pltpu.VMEM((6, 8, 128), F32),
                pltpu.VMEM(doc_ids.shape, jnp.int32),
                dma((10,)),
                dma((4,)), dma((4,)),
                dma((4,)), dma((4,)),
                dma((3,)), dma((3,)),
                dma((5,)), dma((5,)),
                dma, dma,
                dma((6,)), dma((6,)),
                dma((4,)), dma((4,)),
                dma((4, 2 * (planes - 1))), dma((4, planes)),
                dma((4,)), dma((4,)),
                dma((4,)), dma((4,)),
                dma((2,)), dma((2,)),
            ],
            compiler_params=pltpu.CompilerParams(
                collective_id=0, has_side_effects=True, vmem_limit_bytes=48 * 1024 * 1024
            ),
        )(*pinned, token_counts)
    )
    return tuple(
        pl.pallas_call(
            write_kernel,
            out_shape=tuple(jax.ShapeDtypeStruct(a.shape, a.dtype) for a in results),
            in_specs=[pl.BlockSpec(memory_space=pltpu.VMEM)] * 2,
            out_specs=(hbm, hbm),
            scratch_shapes=[dma((4,))],
        )(*(pltpu.with_memory_space_constraint(a, pltpu.VMEM) for a in results))
    )


def solution(mesh):
    in_specs = (
        P("dp", None),
        P("dp", "tensor"),
        P("dp", "tensor"),
        P("dp", "tensor"),
        P("dp", "tensor"),
        P("dp", None),
        P("dp"),
    )
    out_specs = (P("dp", "tensor"), P("dp", "tensor"))
    planes = mesh.shape["tensor"]
    small = (mesh.shape["dp"], planes) == (8, 4)
    body = functools.partial(fused, planes) if small else plain
    return jax.shard_map(body, mesh=mesh, in_specs=in_specs, out_specs=out_specs, check_vma=False)
```

```python
import functools
import math

import jax
import jax.numpy as jnp
from jax import lax
from jax.experimental import pallas as pl
from jax.experimental.pallas import tpu as pltpu
from jax.sharding import PartitionSpec as P

QUERY_HEADS = 64
KEY_VALUE_HEADS = 8
HEAD_SIZE = 128
GROUP = QUERY_HEADS // KEY_VALUE_HEADS
PIECE = 64
MESH = pl.DeviceIdType.MESH
F32 = jnp.float32
BF16 = jnp.bfloat16


def plain(hidden_in, queries, keys, value_weight, context_grad, doc_ids, token_counts):
    tok_rows = hidden_in.shape[0]
    kv_cols = keys.shape[1]
    kv_local = kv_cols // HEAD_SIZE
    scale = 1.0 / math.sqrt(HEAD_SIZE)
    whole = lax.all_gather(value_weight, "dp", axis=0, tiled=True)
    value_states = jnp.dot(hidden_in, whole, preferred_element_type=F32).astype(BF16)
    query_four_axes = queries.reshape(tok_rows, kv_local, GROUP, HEAD_SIZE)
    key_three_axes = keys.reshape(tok_rows, kv_local, HEAD_SIZE)
    scores = (
        jnp.einsum("ikgd,jkd->kgij", query_four_axes, key_three_axes, preferred_element_type=F32)
        * scale
    )
    position = jnp.arange(tok_rows, dtype=jnp.int32)
    doc_here = doc_ids[0]
    allowed = (position[None, :] <= position[:, None]) & (doc_here[:, None] == doc_here[None, :])
    scores = jnp.where(allowed, scores, -jnp.inf)
    top = jnp.max(scores, axis=-1, keepdims=True)
    expo = jnp.exp(scores - top)
    probs = (expo / jnp.sum(expo, axis=-1, keepdims=True)).astype(BF16)
    value_three_axes = value_states.reshape(tok_rows, kv_local, HEAD_SIZE)
    ctx = jnp.einsum("kgij,jkd->ikgd", probs, value_three_axes, preferred_element_type=F32)
    context = ctx.astype(BF16).reshape(tok_rows, kv_local * GROUP * HEAD_SIZE)
    count_here = token_counts[0]
    valid = position < count_here
    masked = jnp.where(valid[:, None], context_grad, jnp.zeros_like(context_grad))
    masked = masked.reshape(tok_rows, kv_local, GROUP, HEAD_SIZE)
    value_gradient = jnp.einsum("kgij,ikgd->jkd", probs, masked, preferred_element_type=F32)
    value_gradient = value_gradient.astype(BF16).reshape(tok_rows, kv_cols)
    count_float = count_here.astype(F32)
    factor = count_float / lax.psum(count_float, "dp")
    full_term = (
        jnp.einsum("tr,tc->rc", hidden_in, value_gradient, preferred_element_type=F32) * factor
    )
    grad = lax.psum_scatter(full_term, "dp", scatter_dimension=0, tiled=True)
    return (context, grad)


def dot_tt(a, b):
    return lax.dot_general(a, b, (((0,), (0,)), ((), ())), preferred_element_type=F32)


def fused_kernel(
    x_hbm, q_hbm, k_hbm, w_hbm, g_hbm, doc_hbm, cnt_ref, ctx, dw_ref,
    x, xp, xfd, xfn, xqd, xqn, q, k, g, wg, pt, bias, dv, dvp, dvn, xd, xn, vown, vsend, vrecv, pf, pfr, ps, pr,
    sendbuf, recvbuf, acc, cnts, doc_ref,
    lsem, xs, xr, ws, wr, cs, cr, ds, dr, vs, vr, ss, sr, ns, nr, zs, zr, fs, fr, qs, qr, us, ur,
):
    me = lax.axis_index("dp")
    plane = lax.axis_index("tensor")
    planes = zr.shape[1]
    core = lax.rem(me, 2)
    chip = me // 2
    cx = lax.rem(chip, 2)
    cy = chip // 2
    peer = me + 1 - 2 * core
    T, C = k.shape
    R = w_hbm.shape[0]
    S = R - xd.shape[2]
    kv = C // HEAD_SIZE
    scale = 1.0 / math.sqrt(HEAD_SIZE)

    def chip_at(rel):
        ax = 1 - cx if rel % 2 else cx
        ay = 1 - cy if rel // 2 else cy
        return 2 * ay + ax

    def same(rel):
        return 2 * chip_at(rel) + core

    def cross(rel):
        return 2 * chip_at(rel) + 1 - core

    lk = pltpu.make_async_copy(k_hbm, k, lsem.at[0])
    lq = pltpu.make_async_copy(q_hbm, q, lsem.at[1])
    lg = pltpu.make_async_copy(g_hbm, g, lsem.at[2])
    lx = pltpu.make_async_copy(x_hbm, x, lsem.at[3])
    lw = pltpu.make_async_copy(w_hbm, wg.at[0], lsem.at[4])
    ld = pltpu.make_async_copy(doc_hbm, doc_ref, lsem.at[5])
    near = (3, 1)
    spans = ((S, R - S), (0, R))
    got, fetch, passed = (xd, xn), (xfd, xfn), (xqd, xqn)
    first_row = pl.multiple_of(plane * PIECE, 16)
    fetched = []
    for a, n in enumerate(near):
        for j, block in enumerate((same(n), cross(n))):
            cols = pl.ds(pl.multiple_of(block * R + spans[a][0], 128), spans[a][1])
            fetched.append(
                pltpu.make_async_copy(
                    x_hbm.at[pl.ds(first_row, PIECE), cols], fetch[a].at[j],
                    lsem.at[6 + 2 * a + j],
                )
            )
    for c in fetched + [lw, ld, lk, lq, lg, lx]:
        c.start()

    bar = pltpu.get_barrier_semaphore()
    others = (peer, same(1), same(2), same(3))
    for d in others:
        pl.semaphore_signal(bar, inc=1, device_id={"dp": d}, device_id_type=MESH)

    @pl.when(plane > 0)
    def _():
        pl.semaphore_signal(bar, inc=1, device_id={"tensor": plane - 1}, device_id_type=MESH)

    @pl.when(plane < planes - 1)
    def _():
        pl.semaphore_signal(bar, inc=1, device_id={"tensor": plane + 1}, device_id_type=MESH)

    inner = (plane > 0) & (plane < planes - 1)
    pl.semaphore_wait(bar, len(others) + 1 + inner.astype(jnp.int32))

    def remote(src, dst, s, r, dev):
        c = pltpu.make_async_remote_copy(
            src_ref=src, dst_ref=dst, send_sem=s, recv_sem=r,
            device_id={"dp": dev}, device_id_type=MESH,
        )
        c.start()
        return c

    for c in fetched:
        c.wait()
    swaps = [remote(fetch[a].at[1], passed[a], us.at[a], ur.at[a], peer) for a in (0, 1)]
    rows = pl.ds(first_row, PIECE)

    def direct(a, j):
        return remote(
            passed[a] if j else fetch[a].at[0], got[a].at[j, rows, :],
            ns.at[2 * a + j], nr.at[2 * a + j], same(near[a]),
        )

    directs = [direct(a, 0) for a in (0, 1)]
    for a in (0, 1):
        swaps[a].wait_recv()
        directs.append(direct(a, 1))
    lw.wait()
    upper, lower = pl.ds(0, S), pl.ds(S, R - S)
    w0 = remote(wg.at[0, upper], wg.at[2, upper], ws.at[0], wr.at[0], same(2))
    w1 = remote(wg.at[0, lower], wg.at[2, lower], ws.at[1], wr.at[1], same(2))
    count = cnt_ref[0].astype(F32)
    cnts[0] = jnp.full(cnts.shape[1:], count, F32)
    c0 = remote(cnts.at[0], cnts.at[1], cs.at[0], cr.at[0], peer)
    xcopies = []
    for i, (rel, size) in enumerate(((3, S), (0, R), (2, R))):
        cols = pl.ds(pl.multiple_of(cross(rel) * R, R), size)
        xcopies.append(
            remote(x_hbm.at[:, cols], xp.at[rel, :, pl.ds(0, size)], xs.at[i], xr.at[i], peer)
        )

    def zcopy(a, j, piece, to, slot):
        here = got[a].at[j, pl.ds(pl.multiple_of(piece * PIECE, 16), PIECE), :]
        return pltpu.make_async_remote_copy(
            src_ref=here, dst_ref=here,
            send_sem=zs.at[2 * a + j, slot], recv_sem=zr.at[2 * a + j, piece],
            device_id={"tensor": to}, device_id_type=MESH,
        )

    def zmoves(step):
        down, up = plane + step, plane - step
        return (
            (down, plane - 1, (plane > 0) & (down < planes), 2 * step),
            (up, plane + 1, (plane < planes - 1) & (up >= 0), 2 * step + 1),
        )

    def spread(a, j):
        directs[2 * j + a].wait_recv()
        for piece, to, has, slot in zmoves(0):
            @pl.when(has)
            def _(piece=piece, to=to, slot=slot):
                zcopy(a, j, piece, to, slot).start()

    def zstep(step, a, js=(0, 1)):
        for j in js:
            for piece, to, has, slot in zmoves(step):
                @pl.when((piece >= 0) & (piece < planes))
                def _(piece=piece):
                    zcopy(a, j, piece, 0, 0).wait_recv()

                if step < planes - 1:
                    @pl.when(has)
                    def _(piece=piece, to=to, slot=slot):
                        zcopy(a, j, piece, to, slot).start()

    def xsent():
        for step in range(planes - 1):
            for piece, to, has, slot in zmoves(step):
                @pl.when(has)
                def _(piece=piece, to=to, slot=slot):
                    for a in (0, 1):
                        for j in (0, 1):
                            zcopy(a, j, piece, to, slot).wait_send()

    ld.wait()
    docs = jnp.broadcast_to(doc_ref[...].astype(F32), (T, T))
    jj = lax.broadcasted_iota(jnp.int32, (T, T), 0)
    ii = lax.broadcasted_iota(jnp.int32, (T, T), 1)
    allowed = (jj <= ii) & (docs == docs.T)
    bias[...] = jnp.where(allowed, 0.0, -jnp.inf).astype(F32)
    lk.wait()
    lq.wait()
    lg.wait()
    row = lax.broadcasted_iota(jnp.int32, (T, HEAD_SIZE), 0).astype(F32)

    def group(kh, _):
        kcols = pl.ds(pl.multiple_of(kh * HEAD_SIZE, HEAD_SIZE), HEAD_SIZE)
        keyg = k[:, kcols]
        total = jnp.zeros((T, HEAD_SIZE), F32)
        for h in range(GROUP):
            cols = pl.ds(pl.multiple_of((kh * GROUP + h) * HEAD_SIZE, HEAD_SIZE), HEAD_SIZE)
            st = lax.dot_general(
                keyg, q[:, cols], (((1,), (1,)), ((), ())), preferred_element_type=F32
            )
            st = st * scale + bias[...]
            e = jnp.exp(st - jnp.max(st, axis=0, keepdims=True))
            p = (e * (1.0 / jnp.sum(e, axis=0, keepdims=True))).astype(BF16)
            pt[kh * GROUP + h] = p
            gm = jnp.where(row < count, g[:, cols].astype(F32), 0.0).astype(BF16)
            total = total + jnp.dot(p, gm, preferred_element_type=F32)
        dv[:, kcols] = (total * count).astype(BF16)
        return 0

    lax.fori_loop(0, kv, group, 0)
    dcopies = [
        remote(dv, dvp, ds.at[0], dr.at[0], peer),
        remote(dv, dvn.at[1, 0], ds.at[1], dr.at[1], same(1)),
    ]
    spread(0, 0)
    spread(1, 0)
    spread(0, 1)
    c0.wait_recv()
    cnts[2] = cnts[0] + cnts[1]
    c1 = remote(cnts.at[2], cnts.at[3], cs.at[1], cr.at[1], same(1))
    lx.wait()
    for c in xcopies:
        c.wait_recv()
    dcopies[0].wait_recv()
    step = 256

    def partial(rel, first, size, store):
        base = same(rel) * R

        def body(t, _):
            off = pl.multiple_of(first + t * step, step)
            xa = x[:, pl.ds(pl.multiple_of(base + off, step), step)]
            xb = xp[rel, :, pl.ds(off, step)]
            store(off, dot_tt(xa, dv[...]) + dot_tt(xb, dvp[...]))
            return 0

        lax.fori_loop(0, size // step, body, 0)

    def send_block(slot, first, size, i, to):
        here = pl.ds(first, size)
        return remote(
            sendbuf.at[slot, here], recvbuf.at[slot, here], ss.at[i], sr.at[i], same(to)
        )

    def fill(slot, rel, first, size, add=None):
        def put(off, val):
            here = pl.ds(off, step)
            if add is not None:
                val = val + recvbuf[add, here, :].astype(F32)
            sendbuf[slot, here, :] = val.astype(BF16)

        partial(rel, first, size, put)

    def keep(off, val):
        acc[pl.ds(off, step), :] = val

    def value_part(rel, size, first=False):
        cols = pl.ds(pl.multiple_of(same(rel) * R, R), size)
        wpart = wg[rel, pl.ds(0, size), :]
        a = jnp.dot(x[:, cols], wpart, preferred_element_type=F32)
        b = jnp.dot(xp[rel, :, pl.ds(0, size)], wpart, preferred_element_type=F32)
        if first:
            vown[...] = a
            vsend[...] = b
        else:
            vown[...] += a
            vsend[...] += b

    late = jnp.where(plane < planes // 2, T - PIECE, 0)
    early = jnp.where(plane < planes // 2, 0, PIECE)
    goes = (
        pl.ds(pl.multiple_of(early, 16), T - PIECE),
        pl.ds(pl.multiple_of(late, 16), PIECE),
    )
    pcopies, qcopies = {}, {}

    def partial_value(a, go):
        here = goes[go]
        i = 2 * go + a
        wpart = wg[0, pl.ds(*spans[a]), :]
        pf[a, 1, here, :] = jnp.dot(got[a][1, here, :], wpart, preferred_element_type=F32)
        pcopies[i] = remote(pf.at[a, 1, here, :], pfr.at[a, here, :], fs.at[i], fr.at[i], peer)
        pf[a, 0, here, :] = jnp.dot(got[a][0, here, :], wpart, preferred_element_type=F32)

    def return_value(a, go):
        here = goes[go]
        i = 2 * go + a
        pcopies[i].wait_recv()
        val = pf[a, 0, here, :] + pfr[a, here, :]
        if a:
            qcopies[2 * go].wait_recv()
            val = val + pr[0, here, :].astype(F32)
        ps[a, here, :] = val.astype(BF16)
        qcopies[i] = remote(
            ps.at[a, here, :], pr.at[a, here, :], qs.at[i], qr.at[i], same(1 if a else 2)
        )

    scopies = []
    for i in range(S // step):
        fill(0, 3, i * step, step)
        scopies.append(send_block(0, i * step, step, i, 1))

    def merge(i):
        scopies[i].wait_recv()
        fill(1, 2, i * step, step, add=0)
        scopies.append(send_block(1, i * step, step, 4 + i, 2))

    zstep(1, 0, (0,))
    spread(1, 1)
    zstep(1, 0, (1,))
    fill(1, 2, S, R - S)
    scopies.append(send_block(1, S, R - S, 3, 2))
    partial(0, 0, S, keep)
    zstep(1, 1, (0,))
    w0.wait_recv()
    w2 = remote(wg.at[2, upper], wg.at[3, upper], ws.at[2], wr.at[2], same(1))
    dcopies[1].wait_recv()
    dcopies.append(remote(dvn.at[1, 0], dvn.at[0, 0], ds.at[2], dr.at[2], same(2)))
    dcopies.append(remote(dvn.at[1, 0], dvn.at[1, 1], ds.at[3], dr.at[3], peer))
    zstep(2, 0)
    partial_value(0, 0)
    zstep(1, 1, (1,))
    return_value(0, 0)
    merge(0)
    zstep(3, 0)
    partial_value(0, 1)
    zstep(2, 1, (0,))
    return_value(0, 1)
    merge(1)
    c1.wait_recv()
    cnts[4] = cnts[2] + cnts[3]
    c2 = remote(cnts.at[4], cnts.at[5], cs.at[2], cr.at[2], same(2))
    merge(2)
    zstep(2, 1, (1,))
    partial_value(1, 0)
    partial(0, S, R - S, keep)
    value_part(0, R, True)
    return_value(1, 0)
    w1.wait_recv()
    value_part(2, R)
    dcopies[2].wait_recv()
    dcopies.append(remote(dvn.at[0, 0], dvn.at[0, 1], ds.at[4], dr.at[4], peer))

    def neighbour_part(a):
        dcopies[4 - a].wait_recv()
        for i in range(spans[a][1] // step):
            cols = pl.ds(i * step, step)
            here = pl.ds(spans[a][0] + i * step, step)
            acc[here, :] += dot_tt(got[a][0, :, cols], dvn[a, 0]) + dot_tt(
                got[a][1, :, cols], dvn[a, 1]
            )

    neighbour_part(0)
    zstep(3, 1)
    partial_value(1, 1)
    return_value(1, 1)
    w2.wait_recv()
    value_part(3, S)
    vcopy = remote(vsend, vrecv, vs, vr, peer)
    neighbour_part(1)
    vcopy.wait_recv()
    vown[...] += vrecv[...]
    c2.wait_recv()
    inv = 1.0 / (cnts[4] + cnts[5])[0:1, 0:1]
    def contexts(first, count):
        rows = pl.ds(first, count)

        def body(kh, _):
            kcols = pl.ds(pl.multiple_of(kh * HEAD_SIZE, HEAD_SIZE), HEAD_SIZE)
            val = vown[:, kcols].astype(BF16)
            for h in range(GROUP):
                head = kh * GROUP + h
                cols = pl.ds(pl.multiple_of(head * HEAD_SIZE, HEAD_SIZE), HEAD_SIZE)
                ctx[rows, cols] = dot_tt(pt[head, :, rows], val).astype(BF16)
            return 0

        lax.fori_loop(0, kv, body, 0)

    def add_values(go):
        qcopies[2 * go + 1].wait_recv()
        vown[goes[go], :] += pr[1, goes[go], :].astype(F32)

    add_values(0)

    @pl.when(plane < planes // 2)
    def _():
        contexts(0, T // 2)

    add_values(1)

    @pl.when(plane >= planes // 2)
    def _():
        contexts(0, T // 2)

    contexts(T // 2, T // 2)

    for i, first, size in ((3, S, R - S), (4, 0, step), (5, step, step), (6, 2 * step, step)):
        scopies[i].wait_recv()
        here = pl.ds(first, size)
        dw_ref[here, :] = (acc[here, :] + recvbuf[1, here, :].astype(F32)) * inv
    xsent()
    partials = list(pcopies.values()) + list(qcopies.values())
    waits = swaps + directs + xcopies + dcopies + scopies + partials
    for c in [w0, w1, w2, vcopy, c0, c1, c2] + waits:
        c.wait_send()


def write_kernel(ctx, dw, ctx_hbm, dw_hbm, sems):
    copies = []
    for src, dst in ((ctx, ctx_hbm), (dw, dw_hbm)):
        rows = src.shape[0] // 2
        for part in range(2):
            here = pl.ds(part * rows, rows)
            copies.append(
                pltpu.make_async_copy(src.at[here], dst.at[here], sems.at[len(copies)])
            )
    for c in copies:
        c.start()
    for c in copies:
        c.wait()


def fused(planes, hidden_in, queries, keys, value_weight, context_grad, doc_ids, token_counts):
    T, M = hidden_in.shape
    C = keys.shape[1]
    Q = queries.shape[1]
    R = value_weight.shape[0]
    heads = Q // HEAD_SIZE
    hbm = pl.BlockSpec(memory_space=pltpu.HBM)
    dma = pltpu.SemaphoreType.DMA
    pinned = [
        pltpu.with_memory_space_constraint(a, pltpu.HBM)
        for a in (hidden_in, queries, keys, value_weight, context_grad, doc_ids)
    ]
    results = tuple(
        pl.pallas_call(
            fused_kernel,
            out_shape=(
                jax.ShapeDtypeStruct((T, Q), BF16),
                jax.ShapeDtypeStruct((R, C), F32),
            ),
            in_specs=[hbm] * 6 + [pl.BlockSpec(memory_space=pltpu.SMEM)],
            out_specs=(pl.BlockSpec(memory_space=pltpu.VMEM),) * 2,
            scratch_shapes=[
                pltpu.VMEM((T, M), BF16),
                pltpu.VMEM((4, T, R), BF16),
                pltpu.VMEM((2, PIECE, R // 4), BF16),
                pltpu.VMEM((2, PIECE, R), BF16),
                pltpu.VMEM((PIECE, R // 4), BF16),
                pltpu.VMEM((PIECE, R), BF16),
                pltpu.VMEM((T, Q), BF16),
                pltpu.VMEM((T, C), BF16),
                pltpu.VMEM((T, Q), BF16),
                pltpu.VMEM((4, R, C), BF16),
                pltpu.VMEM((heads, T, T), BF16),
                pltpu.VMEM((T, T), F32),
                pltpu.VMEM((T, C), BF16),
                pltpu.VMEM((T, C), BF16),
                pltpu.VMEM((2, 2, T, C), BF16),
                pltpu.VMEM((2, T, R // 4), BF16),
                pltpu.VMEM((2, T, R), BF16),
                pltpu.VMEM((T, C), F32),
                pltpu.VMEM((T, C), F32),
                pltpu.VMEM((T, C), F32),
                pltpu.VMEM((2, 2, T, C), F32),
                pltpu.VMEM((2, T, C), F32),
                pltpu.VMEM((2, T, C), BF16),
                pltpu.VMEM((2, T, C), BF16),
                pltpu.VMEM((2, R, C), BF16),
                pltpu.VMEM((2, R, C), BF16),
                pltpu.VMEM((R, C), F32),
                pltpu.VMEM((6, 8, 128), F32),
                pltpu.VMEM(doc_ids.shape, jnp.int32),
                dma((10,)),
                dma((4,)), dma((4,)),
                dma((4,)), dma((4,)),
                dma((3,)), dma((3,)),
                dma((5,)), dma((5,)),
                dma, dma,
                dma((7,)), dma((7,)),
                dma((4,)), dma((4,)),
                dma((4, 2 * (planes - 1))), dma((4, planes)),
                dma((4,)), dma((4,)),
                dma((4,)), dma((4,)),
                dma((2,)), dma((2,)),
            ],
            compiler_params=pltpu.CompilerParams(
                collective_id=0, has_side_effects=True, vmem_limit_bytes=48 * 1024 * 1024
            ),
        )(*pinned, token_counts)
    )
    return tuple(
        pl.pallas_call(
            write_kernel,
            out_shape=tuple(jax.ShapeDtypeStruct(a.shape, a.dtype) for a in results),
            in_specs=[pl.BlockSpec(memory_space=pltpu.VMEM)] * 2,
            out_specs=(hbm, hbm),
            scratch_shapes=[dma((4,))],
        )(*(pltpu.with_memory_space_constraint(a, pltpu.VMEM) for a in results))
    )


def solution(mesh):
    in_specs = (
        P("dp", None),
        P("dp", "tensor"),
        P("dp", "tensor"),
        P("dp", "tensor"),
        P("dp", "tensor"),
        P("dp", None),
        P("dp"),
    )
    out_specs = (P("dp", "tensor"), P("dp", "tensor"))
    planes = mesh.shape["tensor"]
    small = (mesh.shape["dp"], planes) == (8, 4)
    body = functools.partial(fused, planes) if small else plain
    return jax.shard_map(body, mesh=mesh, in_specs=in_specs, out_specs=out_specs, check_vma=False)
```

```python
import functools
import math

import jax
import jax.numpy as jnp
from jax import lax
from jax.experimental import pallas as pl
from jax.experimental.pallas import tpu as pltpu
from jax.sharding import PartitionSpec as P

QUERY_HEADS = 64
KEY_VALUE_HEADS = 8
HEAD_SIZE = 128
GROUP = QUERY_HEADS // KEY_VALUE_HEADS
PIECE = 64
MESH = pl.DeviceIdType.MESH
F32 = jnp.float32
BF16 = jnp.bfloat16


def plain(hidden_in, queries, keys, value_weight, context_grad, doc_ids, token_counts):
    tok_rows = hidden_in.shape[0]
    kv_cols = keys.shape[1]
    kv_local = kv_cols // HEAD_SIZE
    scale = 1.0 / math.sqrt(HEAD_SIZE)
    whole = lax.all_gather(value_weight, "dp", axis=0, tiled=True)
    value_states = jnp.dot(hidden_in, whole, preferred_element_type=F32).astype(BF16)
    query_four_axes = queries.reshape(tok_rows, kv_local, GROUP, HEAD_SIZE)
    key_three_axes = keys.reshape(tok_rows, kv_local, HEAD_SIZE)
    scores = (
        jnp.einsum("ikgd,jkd->kgij", query_four_axes, key_three_axes, preferred_element_type=F32)
        * scale
    )
    position = jnp.arange(tok_rows, dtype=jnp.int32)
    doc_here = doc_ids[0]
    allowed = (position[None, :] <= position[:, None]) & (doc_here[:, None] == doc_here[None, :])
    scores = jnp.where(allowed, scores, -jnp.inf)
    top = jnp.max(scores, axis=-1, keepdims=True)
    expo = jnp.exp(scores - top)
    probs = (expo / jnp.sum(expo, axis=-1, keepdims=True)).astype(BF16)
    value_three_axes = value_states.reshape(tok_rows, kv_local, HEAD_SIZE)
    ctx = jnp.einsum("kgij,jkd->ikgd", probs, value_three_axes, preferred_element_type=F32)
    context = ctx.astype(BF16).reshape(tok_rows, kv_local * GROUP * HEAD_SIZE)
    count_here = token_counts[0]
    valid = position < count_here
    masked = jnp.where(valid[:, None], context_grad, jnp.zeros_like(context_grad))
    masked = masked.reshape(tok_rows, kv_local, GROUP, HEAD_SIZE)
    value_gradient = jnp.einsum("kgij,ikgd->jkd", probs, masked, preferred_element_type=F32)
    value_gradient = value_gradient.astype(BF16).reshape(tok_rows, kv_cols)
    count_float = count_here.astype(F32)
    factor = count_float / lax.psum(count_float, "dp")
    full_term = (
        jnp.einsum("tr,tc->rc", hidden_in, value_gradient, preferred_element_type=F32) * factor
    )
    grad = lax.psum_scatter(full_term, "dp", scatter_dimension=0, tiled=True)
    return (context, grad)


def dot_tt(a, b):
    return lax.dot_general(a, b, (((0,), (0,)), ((), ())), preferred_element_type=F32)


def fused_kernel(
    x_hbm, q_hbm, k_hbm, w_hbm, g_hbm, doc_hbm, cnt_ref, ctx, dw_ref,
    x, xp, xfd, xfn, xqd, xqn, q, k, g, wg, pt, bias, dv, dvp, dvn, xd, xn, vown, vsend, vrecv, pf, pfr, ps, pr,
    sendbuf, recvbuf, acc, cnts, doc_ref,
    lsem, xs, xr, ws, wr, cs, cr, ds, dr, vs, vr, ss, sr, ns, nr, zs, zr, fs, fr, qs, qr, us, ur,
):
    me = lax.axis_index("dp")
    plane = lax.axis_index("tensor")
    planes = zr.shape[1]
    core = lax.rem(me, 2)
    chip = me // 2
    cx = lax.rem(chip, 2)
    cy = chip // 2
    peer = me + 1 - 2 * core
    T, C = k.shape
    R = w_hbm.shape[0]
    S = R - xd.shape[2]
    kv = C // HEAD_SIZE
    scale = 1.0 / math.sqrt(HEAD_SIZE)

    def chip_at(rel):
        ax = 1 - cx if rel % 2 else cx
        ay = 1 - cy if rel // 2 else cy
        return 2 * ay + ax

    def same(rel):
        return 2 * chip_at(rel) + core

    def cross(rel):
        return 2 * chip_at(rel) + 1 - core

    lk = pltpu.make_async_copy(k_hbm, k, lsem.at[0])
    lq = pltpu.make_async_copy(q_hbm, q, lsem.at[1])
    lg = pltpu.make_async_copy(g_hbm, g, lsem.at[2])
    lx = pltpu.make_async_copy(x_hbm, x, lsem.at[3])
    lw = pltpu.make_async_copy(w_hbm, wg.at[0], lsem.at[4])
    ld = pltpu.make_async_copy(doc_hbm, doc_ref, lsem.at[5])
    near = (3, 1)
    spans = ((S, R - S), (0, R))
    got, fetch, passed = (xd, xn), (xfd, xfn), (xqd, xqn)
    first_row = pl.multiple_of(plane * PIECE, 16)
    fetched = []
    for a, n in enumerate(near):
        for j, block in enumerate((same(n), cross(n))):
            cols = pl.ds(pl.multiple_of(block * R + spans[a][0], 128), spans[a][1])
            fetched.append(
                pltpu.make_async_copy(
                    x_hbm.at[pl.ds(first_row, PIECE), cols], fetch[a].at[j],
                    lsem.at[6 + 2 * a + j],
                )
            )
    for c in fetched + [lw, ld, lk, lq, lg, lx]:
        c.start()

    bar = pltpu.get_barrier_semaphore()
    others = (peer, same(1), same(2), same(3))
    for d in others:
        pl.semaphore_signal(bar, inc=1, device_id={"dp": d}, device_id_type=MESH)

    @pl.when(plane > 0)
    def _():
        pl.semaphore_signal(bar, inc=1, device_id={"tensor": plane - 1}, device_id_type=MESH)

    @pl.when(plane < planes - 1)
    def _():
        pl.semaphore_signal(bar, inc=1, device_id={"tensor": plane + 1}, device_id_type=MESH)

    inner = (plane > 0) & (plane < planes - 1)
    pl.semaphore_wait(bar, len(others) + 1 + inner.astype(jnp.int32))

    def remote(src, dst, s, r, dev):
        c = pltpu.make_async_remote_copy(
            src_ref=src, dst_ref=dst, send_sem=s, recv_sem=r,
            device_id={"dp": dev}, device_id_type=MESH,
        )
        c.start()
        return c

    for c in fetched:
        c.wait()
    swaps = [remote(fetch[a].at[1], passed[a], us.at[a], ur.at[a], peer) for a in (0, 1)]
    rows = pl.ds(first_row, PIECE)

    def direct(a, j):
        return remote(
            passed[a] if j else fetch[a].at[0], got[a].at[j, rows, :],
            ns.at[2 * a + j], nr.at[2 * a + j], same(near[a]),
        )

    directs = [direct(a, 0) for a in (0, 1)]
    for a in (0, 1):
        swaps[a].wait_recv()
        directs.append(direct(a, 1))
    lw.wait()
    upper, lower = pl.ds(0, S), pl.ds(S, R - S)
    w0 = remote(wg.at[0, upper], wg.at[2, upper], ws.at[0], wr.at[0], same(2))
    w1 = remote(wg.at[0, lower], wg.at[2, lower], ws.at[1], wr.at[1], same(2))
    count = cnt_ref[0].astype(F32)
    cnts[0] = jnp.full(cnts.shape[1:], count, F32)
    c0 = remote(cnts.at[0], cnts.at[1], cs.at[0], cr.at[0], peer)
    xcopies = []
    for i, (rel, size) in enumerate(((3, S), (0, R), (2, R))):
        cols = pl.ds(pl.multiple_of(cross(rel) * R, R), size)
        xcopies.append(
            remote(x_hbm.at[:, cols], xp.at[rel, :, pl.ds(0, size)], xs.at[i], xr.at[i], peer)
        )

    def zcopy(a, j, piece, to, slot):
        here = got[a].at[j, pl.ds(pl.multiple_of(piece * PIECE, 16), PIECE), :]
        return pltpu.make_async_remote_copy(
            src_ref=here, dst_ref=here,
            send_sem=zs.at[2 * a + j, slot], recv_sem=zr.at[2 * a + j, piece],
            device_id={"tensor": to}, device_id_type=MESH,
        )

    def zmoves(step):
        down, up = plane + step, plane - step
        return (
            (down, plane - 1, (plane > 0) & (down < planes), 2 * step),
            (up, plane + 1, (plane < planes - 1) & (up >= 0), 2 * step + 1),
        )

    def spread(a, j):
        directs[2 * j + a].wait_recv()
        for piece, to, has, slot in zmoves(0):
            @pl.when(has)
            def _(piece=piece, to=to, slot=slot):
                zcopy(a, j, piece, to, slot).start()

    def zstep(step, a, js=(0, 1)):
        for j in js:
            for piece, to, has, slot in zmoves(step):
                @pl.when((piece >= 0) & (piece < planes))
                def _(piece=piece):
                    zcopy(a, j, piece, 0, 0).wait_recv()

                if step < planes - 1:
                    @pl.when(has)
                    def _(piece=piece, to=to, slot=slot):
                        zcopy(a, j, piece, to, slot).start()

    def xsent():
        for step in range(planes - 1):
            for piece, to, has, slot in zmoves(step):
                @pl.when(has)
                def _(piece=piece, to=to, slot=slot):
                    for a in (0, 1):
                        for j in (0, 1):
                            zcopy(a, j, piece, to, slot).wait_send()

    ld.wait()
    docs = jnp.broadcast_to(doc_ref[...].astype(F32), (T, T))
    jj = lax.broadcasted_iota(jnp.int32, (T, T), 0)
    ii = lax.broadcasted_iota(jnp.int32, (T, T), 1)
    allowed = (jj <= ii) & (docs == docs.T)
    bias[...] = jnp.where(allowed, 0.0, -jnp.inf).astype(F32)
    lk.wait()
    lq.wait()
    lg.wait()
    row = lax.broadcasted_iota(jnp.int32, (T, HEAD_SIZE), 0).astype(F32)

    def group(kh, _):
        kcols = pl.ds(pl.multiple_of(kh * HEAD_SIZE, HEAD_SIZE), HEAD_SIZE)
        keyg = k[:, kcols]
        total = jnp.zeros((T, HEAD_SIZE), F32)
        for h in range(GROUP):
            cols = pl.ds(pl.multiple_of((kh * GROUP + h) * HEAD_SIZE, HEAD_SIZE), HEAD_SIZE)
            st = lax.dot_general(
                keyg, q[:, cols], (((1,), (1,)), ((), ())), preferred_element_type=F32
            )
            st = st * scale + bias[...]
            e = jnp.exp(st - jnp.max(st, axis=0, keepdims=True))
            p = (e * (1.0 / jnp.sum(e, axis=0, keepdims=True))).astype(BF16)
            pt[kh * GROUP + h] = p
            gm = jnp.where(row < count, g[:, cols].astype(F32), 0.0).astype(BF16)
            total = total + jnp.dot(p, gm, preferred_element_type=F32)
        dv[:, kcols] = (total * count).astype(BF16)
        return 0

    lax.fori_loop(0, kv, group, 0)
    dcopies = [
        remote(dv, dvp, ds.at[0], dr.at[0], peer),
        remote(dv, dvn.at[1, 0], ds.at[1], dr.at[1], same(1)),
    ]
    spread(0, 0)
    spread(1, 0)
    spread(0, 1)
    c0.wait_recv()
    cnts[2] = cnts[0] + cnts[1]
    c1 = remote(cnts.at[2], cnts.at[3], cs.at[1], cr.at[1], same(1))
    lx.wait()
    for c in xcopies:
        c.wait_recv()
    dcopies[0].wait_recv()
    step = 256

    def partial(rel, first, size, store):
        base = same(rel) * R

        def body(t, _):
            off = pl.multiple_of(first + t * step, step)
            xa = x[:, pl.ds(pl.multiple_of(base + off, step), step)]
            xb = xp[rel, :, pl.ds(off, step)]
            store(off, dot_tt(xa, dv[...]) + dot_tt(xb, dvp[...]))
            return 0

        lax.fori_loop(0, size // step, body, 0)

    def send_block(slot, first, size, i, to):
        here = pl.ds(first, size)
        return remote(
            sendbuf.at[slot, here], recvbuf.at[slot, here], ss.at[i], sr.at[i], same(to)
        )

    def fill(slot, rel, first, size, add=None):
        def put(off, val):
            here = pl.ds(off, step)
            if add is not None:
                val = val + recvbuf[add, here, :].astype(F32)
            sendbuf[slot, here, :] = val.astype(BF16)

        partial(rel, first, size, put)

    def keep(off, val):
        acc[pl.ds(off, step), :] = val

    def value_part(rel, size, first=False):
        cols = pl.ds(pl.multiple_of(same(rel) * R, R), size)
        wpart = wg[rel, pl.ds(0, size), :]
        a = jnp.dot(x[:, cols], wpart, preferred_element_type=F32)
        b = jnp.dot(xp[rel, :, pl.ds(0, size)], wpart, preferred_element_type=F32)
        if first:
            vown[...] = a
            vsend[...] = b
        else:
            vown[...] += a
            vsend[...] += b

    late = jnp.where(plane < planes // 2, T - PIECE, 0)
    early = jnp.where(plane < planes // 2, 0, PIECE)
    goes = (
        pl.ds(pl.multiple_of(early, 16), T - PIECE),
        pl.ds(pl.multiple_of(late, 16), PIECE),
    )
    pcopies, qcopies = {}, {}

    def partial_value(a, go):
        here = goes[go]
        i = 2 * go + a
        wpart = wg[0, pl.ds(*spans[a]), :]
        pf[a, 1, here, :] = jnp.dot(got[a][1, here, :], wpart, preferred_element_type=F32)
        pcopies[i] = remote(pf.at[a, 1, here, :], pfr.at[a, here, :], fs.at[i], fr.at[i], peer)
        pf[a, 0, here, :] = jnp.dot(got[a][0, here, :], wpart, preferred_element_type=F32)

    def return_value(a, go):
        here = goes[go]
        i = 2 * go + a
        pcopies[i].wait_recv()
        val = pf[a, 0, here, :] + pfr[a, here, :]
        if a:
            qcopies[2 * go].wait_recv()
            val = val + pr[0, here, :].astype(F32)
        ps[a, here, :] = val.astype(BF16)
        qcopies[i] = remote(
            ps.at[a, here, :], pr.at[a, here, :], qs.at[i], qr.at[i], same(1 if a else 2)
        )

    scopies = []
    for i in range(S // step):
        fill(0, 3, i * step, step)
        scopies.append(send_block(0, i * step, step, i, 1))

    def merge(i):
        scopies[i].wait_recv()
        fill(1, 2, i * step, step, add=0)
        scopies.append(send_block(1, i * step, step, 4 + i, 2))

    zstep(1, 0, (0,))
    spread(1, 1)
    zstep(1, 0, (1,))
    fill(1, 2, S, R - S)
    scopies.append(send_block(1, S, R - S, 3, 2))
    partial(0, 0, S, keep)
    zstep(1, 1, (0,))
    w0.wait_recv()
    w2 = remote(wg.at[2, upper], wg.at[3, upper], ws.at[2], wr.at[2], same(1))
    dcopies[1].wait_recv()
    dcopies.append(remote(dvn.at[1, 0], dvn.at[0, 0], ds.at[2], dr.at[2], same(2)))
    dcopies.append(remote(dvn.at[1, 0], dvn.at[1, 1], ds.at[3], dr.at[3], peer))
    zstep(2, 0)
    partial_value(0, 0)
    zstep(1, 1, (1,))
    return_value(0, 0)
    merge(0)
    zstep(3, 0)
    partial_value(0, 1)
    zstep(2, 1, (0,))
    return_value(0, 1)
    merge(1)
    c1.wait_recv()
    cnts[4] = cnts[2] + cnts[3]
    c2 = remote(cnts.at[4], cnts.at[5], cs.at[2], cr.at[2], same(2))
    merge(2)
    zstep(2, 1, (1,))
    partial_value(1, 0)
    partial(0, S, R - S, keep)
    value_part(0, R, True)
    return_value(1, 0)
    w1.wait_recv()
    value_part(2, R)
    dcopies[2].wait_recv()
    dcopies.append(remote(dvn.at[0, 0], dvn.at[0, 1], ds.at[4], dr.at[4], peer))

    def neighbour_part(a):
        dcopies[4 - a].wait_recv()
        for i in range(spans[a][1] // step):
            cols = pl.ds(i * step, step)
            here = pl.ds(spans[a][0] + i * step, step)
            acc[here, :] += dot_tt(got[a][0, :, cols], dvn[a, 0]) + dot_tt(
                got[a][1, :, cols], dvn[a, 1]
            )

    neighbour_part(0)
    zstep(3, 1)
    partial_value(1, 1)
    vcopy = pltpu.make_async_remote_copy(
        src_ref=vsend, dst_ref=vrecv, send_sem=vs, recv_sem=vr,
        device_id={"dp": peer}, device_id_type=MESH,
    )

    def end_value():
        w2.wait_recv()
        value_part(3, S)
        vcopy.start()

    @pl.when(core == 1)
    def _():
        end_value()

    return_value(1, 1)

    @pl.when(core == 0)
    def _():
        end_value()

    neighbour_part(1)
    vcopy.wait_recv()
    vown[...] += vrecv[...]
    c2.wait_recv()
    inv = 1.0 / (cnts[4] + cnts[5])[0:1, 0:1]
    def contexts(first, count):
        rows = pl.ds(first, count)

        def body(kh, _):
            kcols = pl.ds(pl.multiple_of(kh * HEAD_SIZE, HEAD_SIZE), HEAD_SIZE)
            val = vown[:, kcols].astype(BF16)
            for h in range(GROUP):
                head = kh * GROUP + h
                cols = pl.ds(pl.multiple_of(head * HEAD_SIZE, HEAD_SIZE), HEAD_SIZE)
                ctx[rows, cols] = dot_tt(pt[head, :, rows], val).astype(BF16)
            return 0

        lax.fori_loop(0, kv, body, 0)

    def add_values(go):
        qcopies[2 * go + 1].wait_recv()
        vown[goes[go], :] += pr[1, goes[go], :].astype(F32)

    add_values(0)

    @pl.when(plane < planes // 2)
    def _():
        contexts(0, T // 2)

    add_values(1)

    @pl.when(plane >= planes // 2)
    def _():
        contexts(0, T // 2)

    contexts(T // 2, T // 2)

    for i, first, size in ((3, S, R - S), (4, 0, step), (5, step, step), (6, 2 * step, step)):
        scopies[i].wait_recv()
        here = pl.ds(first, size)
        dw_ref[here, :] = (acc[here, :] + recvbuf[1, here, :].astype(F32)) * inv
    xsent()
    partials = list(pcopies.values()) + list(qcopies.values())
    waits = swaps + directs + xcopies + dcopies + scopies + partials
    for c in [w0, w1, w2, vcopy, c0, c1, c2] + waits:
        c.wait_send()


def write_kernel(ctx, dw, ctx_hbm, dw_hbm, sems):
    copies = []
    for src, dst in ((ctx, ctx_hbm), (dw, dw_hbm)):
        rows = src.shape[0] // 2
        for part in range(2):
            here = pl.ds(part * rows, rows)
            copies.append(
                pltpu.make_async_copy(src.at[here], dst.at[here], sems.at[len(copies)])
            )
    for c in copies:
        c.start()
    for c in copies:
        c.wait()


def fused(planes, hidden_in, queries, keys, value_weight, context_grad, doc_ids, token_counts):
    T, M = hidden_in.shape
    C = keys.shape[1]
    Q = queries.shape[1]
    R = value_weight.shape[0]
    heads = Q // HEAD_SIZE
    hbm = pl.BlockSpec(memory_space=pltpu.HBM)
    dma = pltpu.SemaphoreType.DMA
    pinned = [
        pltpu.with_memory_space_constraint(a, pltpu.HBM)
        for a in (hidden_in, queries, keys, value_weight, context_grad, doc_ids)
    ]
    results = tuple(
        pl.pallas_call(
            fused_kernel,
            out_shape=(
                jax.ShapeDtypeStruct((T, Q), BF16),
                jax.ShapeDtypeStruct((R, C), F32),
            ),
            in_specs=[hbm] * 6 + [pl.BlockSpec(memory_space=pltpu.SMEM)],
            out_specs=(pl.BlockSpec(memory_space=pltpu.VMEM),) * 2,
            scratch_shapes=[
                pltpu.VMEM((T, M), BF16),
                pltpu.VMEM((4, T, R), BF16),
                pltpu.VMEM((2, PIECE, R // 4), BF16),
                pltpu.VMEM((2, PIECE, R), BF16),
                pltpu.VMEM((PIECE, R // 4), BF16),
                pltpu.VMEM((PIECE, R), BF16),
                pltpu.VMEM((T, Q), BF16),
                pltpu.VMEM((T, C), BF16),
                pltpu.VMEM((T, Q), BF16),
                pltpu.VMEM((4, R, C), BF16),
                pltpu.VMEM((heads, T, T), BF16),
                pltpu.VMEM((T, T), F32),
                pltpu.VMEM((T, C), BF16),
                pltpu.VMEM((T, C), BF16),
                pltpu.VMEM((2, 2, T, C), BF16),
                pltpu.VMEM((2, T, R // 4), BF16),
                pltpu.VMEM((2, T, R), BF16),
                pltpu.VMEM((T, C), F32),
                pltpu.VMEM((T, C), F32),
                pltpu.VMEM((T, C), F32),
                pltpu.VMEM((2, 2, T, C), F32),
                pltpu.VMEM((2, T, C), F32),
                pltpu.VMEM((2, T, C), BF16),
                pltpu.VMEM((2, T, C), BF16),
                pltpu.VMEM((2, R, C), BF16),
                pltpu.VMEM((2, R, C), BF16),
                pltpu.VMEM((R, C), F32),
                pltpu.VMEM((6, 8, 128), F32),
                pltpu.VMEM(doc_ids.shape, jnp.int32),
                dma((10,)),
                dma((4,)), dma((4,)),
                dma((4,)), dma((4,)),
                dma((3,)), dma((3,)),
                dma((5,)), dma((5,)),
                dma, dma,
                dma((7,)), dma((7,)),
                dma((4,)), dma((4,)),
                dma((4, 2 * (planes - 1))), dma((4, planes)),
                dma((4,)), dma((4,)),
                dma((4,)), dma((4,)),
                dma((2,)), dma((2,)),
            ],
            compiler_params=pltpu.CompilerParams(
                collective_id=0, has_side_effects=True, vmem_limit_bytes=48 * 1024 * 1024
            ),
        )(*pinned, token_counts)
    )
    return tuple(
        pl.pallas_call(
            write_kernel,
            out_shape=tuple(jax.ShapeDtypeStruct(a.shape, a.dtype) for a in results),
            in_specs=[pl.BlockSpec(memory_space=pltpu.VMEM)] * 2,
            out_specs=(hbm, hbm),
            scratch_shapes=[dma((4,))],
        )(*(pltpu.with_memory_space_constraint(a, pltpu.VMEM) for a in results))
    )


def solution(mesh):
    in_specs = (
        P("dp", None),
        P("dp", "tensor"),
        P("dp", "tensor"),
        P("dp", "tensor"),
        P("dp", "tensor"),
        P("dp", None),
        P("dp"),
    )
    out_specs = (P("dp", "tensor"), P("dp", "tensor"))
    planes = mesh.shape["tensor"]
    small = (mesh.shape["dp"], planes) == (8, 4)
    body = functools.partial(fused, planes) if small else plain
    return jax.shard_map(body, mesh=mesh, in_specs=in_specs, out_specs=out_specs, check_vma=False)
```

```python
import functools
import math

import jax
import jax.numpy as jnp
from jax import lax
from jax.experimental import pallas as pl
from jax.experimental.pallas import tpu as pltpu
from jax.sharding import PartitionSpec as P

QUERY_HEADS = 64
KEY_VALUE_HEADS = 8
HEAD_SIZE = 128
GROUP = QUERY_HEADS // KEY_VALUE_HEADS
PIECE = 64
MESH = pl.DeviceIdType.MESH
F32 = jnp.float32
BF16 = jnp.bfloat16


def plain(hidden_in, queries, keys, value_weight, context_grad, doc_ids, token_counts):
    tok_rows = hidden_in.shape[0]
    kv_cols = keys.shape[1]
    kv_local = kv_cols // HEAD_SIZE
    scale = 1.0 / math.sqrt(HEAD_SIZE)
    whole = lax.all_gather(value_weight, "dp", axis=0, tiled=True)
    value_states = jnp.dot(hidden_in, whole, preferred_element_type=F32).astype(BF16)
    query_four_axes = queries.reshape(tok_rows, kv_local, GROUP, HEAD_SIZE)
    key_three_axes = keys.reshape(tok_rows, kv_local, HEAD_SIZE)
    scores = (
        jnp.einsum("ikgd,jkd->kgij", query_four_axes, key_three_axes, preferred_element_type=F32)
        * scale
    )
    position = jnp.arange(tok_rows, dtype=jnp.int32)
    doc_here = doc_ids[0]
    allowed = (position[None, :] <= position[:, None]) & (doc_here[:, None] == doc_here[None, :])
    scores = jnp.where(allowed, scores, -jnp.inf)
    top = jnp.max(scores, axis=-1, keepdims=True)
    expo = jnp.exp(scores - top)
    probs = (expo / jnp.sum(expo, axis=-1, keepdims=True)).astype(BF16)
    value_three_axes = value_states.reshape(tok_rows, kv_local, HEAD_SIZE)
    ctx = jnp.einsum("kgij,jkd->ikgd", probs, value_three_axes, preferred_element_type=F32)
    context = ctx.astype(BF16).reshape(tok_rows, kv_local * GROUP * HEAD_SIZE)
    count_here = token_counts[0]
    valid = position < count_here
    masked = jnp.where(valid[:, None], context_grad, jnp.zeros_like(context_grad))
    masked = masked.reshape(tok_rows, kv_local, GROUP, HEAD_SIZE)
    value_gradient = jnp.einsum("kgij,ikgd->jkd", probs, masked, preferred_element_type=F32)
    value_gradient = value_gradient.astype(BF16).reshape(tok_rows, kv_cols)
    count_float = count_here.astype(F32)
    factor = count_float / lax.psum(count_float, "dp")
    full_term = (
        jnp.einsum("tr,tc->rc", hidden_in, value_gradient, preferred_element_type=F32) * factor
    )
    grad = lax.psum_scatter(full_term, "dp", scatter_dimension=0, tiled=True)
    return (context, grad)


def dot_tt(a, b):
    return lax.dot_general(a, b, (((0,), (0,)), ((), ())), preferred_element_type=F32)


def fused_kernel(
    x_hbm, q_hbm, k_hbm, w_hbm, g_hbm, doc_hbm, cnt_ref, ctx, dw_ref,
    x, xp, xfd, xfn, xqd, xqn, q, k, g, wg, pt, bias, dv, dvp, dvn, xd, xn, vown, vsend, vrecv, pf, pfr, ps, pr,
    sendbuf, recvbuf, acc, cnts, doc_ref,
    lsem, xs, xr, ws, wr, cs, cr, ds, dr, vs, vr, ss, sr, ns, nr, zs, zr, fs, fr, qs, qr, us, ur,
):
    me = lax.axis_index("dp")
    plane = lax.axis_index("tensor")
    planes = zr.shape[1]
    core = lax.rem(me, 2)
    chip = me // 2
    cx = lax.rem(chip, 2)
    cy = chip // 2
    peer = me + 1 - 2 * core
    T, C = k.shape
    R = w_hbm.shape[0]
    S = R - xd.shape[2]
    kv = C // HEAD_SIZE
    scale = 1.0 / math.sqrt(HEAD_SIZE)

    def chip_at(rel):
        ax = 1 - cx if rel % 2 else cx
        ay = 1 - cy if rel // 2 else cy
        return 2 * ay + ax

    def same(rel):
        return 2 * chip_at(rel) + core

    def cross(rel):
        return 2 * chip_at(rel) + 1 - core

    lk = pltpu.make_async_copy(k_hbm, k, lsem.at[0])
    lq = pltpu.make_async_copy(q_hbm, q, lsem.at[1])
    lg = pltpu.make_async_copy(g_hbm, g, lsem.at[2])
    lx = pltpu.make_async_copy(x_hbm, x, lsem.at[3])
    lw = pltpu.make_async_copy(w_hbm, wg.at[0], lsem.at[4])
    ld = pltpu.make_async_copy(doc_hbm, doc_ref, lsem.at[5])
    near = (3, 1)
    spans = ((S, R - S), (0, R))
    got, fetch, passed = (xd, xn), (xfd, xfn), (xqd, xqn)
    first_row = pl.multiple_of(plane * PIECE, 16)
    fetched = []
    for a, n in enumerate(near):
        for j, block in enumerate((same(n), cross(n))):
            cols = pl.ds(pl.multiple_of(block * R + spans[a][0], 128), spans[a][1])
            fetched.append(
                pltpu.make_async_copy(
                    x_hbm.at[pl.ds(first_row, PIECE), cols], fetch[a].at[j],
                    lsem.at[6 + 2 * a + j],
                )
            )
    for c in fetched + [lw, ld, lk, lq, lg, lx]:
        c.start()

    bar = pltpu.get_barrier_semaphore()
    others = (peer, same(1), same(2), same(3))
    for d in others:
        pl.semaphore_signal(bar, inc=1, device_id={"dp": d}, device_id_type=MESH)

    @pl.when(plane > 0)
    def _():
        pl.semaphore_signal(bar, inc=1, device_id={"tensor": plane - 1}, device_id_type=MESH)

    @pl.when(plane < planes - 1)
    def _():
        pl.semaphore_signal(bar, inc=1, device_id={"tensor": plane + 1}, device_id_type=MESH)

    inner = (plane > 0) & (plane < planes - 1)
    pl.semaphore_wait(bar, len(others) + 1 + inner.astype(jnp.int32))

    def remote(src, dst, s, r, dev):
        c = pltpu.make_async_remote_copy(
            src_ref=src, dst_ref=dst, send_sem=s, recv_sem=r,
            device_id={"dp": dev}, device_id_type=MESH,
        )
        c.start()
        return c

    for c in fetched:
        c.wait()
    swaps = [remote(fetch[a].at[1], passed[a], us.at[a], ur.at[a], peer) for a in (0, 1)]
    rows = pl.ds(first_row, PIECE)

    def direct(a, j):
        return remote(
            passed[a] if j else fetch[a].at[0], got[a].at[j, rows, :],
            ns.at[2 * a + j], nr.at[2 * a + j], same(near[a]),
        )

    directs = [direct(a, 0) for a in (0, 1)]
    for a in (0, 1):
        swaps[a].wait_recv()
        directs.append(direct(a, 1))
    lw.wait()
    upper, lower = pl.ds(0, S), pl.ds(S, R - S)
    w0 = remote(wg.at[0, upper], wg.at[2, upper], ws.at[0], wr.at[0], same(2))
    w1 = remote(wg.at[0, lower], wg.at[2, lower], ws.at[1], wr.at[1], same(2))
    count = cnt_ref[0].astype(F32)
    cnts[0] = jnp.full(cnts.shape[1:], count, F32)
    c0 = remote(cnts.at[0], cnts.at[1], cs.at[0], cr.at[0], peer)
    xcopies = []
    for i, (rel, size) in enumerate(((3, S), (0, R), (2, R))):
        cols = pl.ds(pl.multiple_of(cross(rel) * R, R), size)
        xcopies.append(
            remote(x_hbm.at[:, cols], xp.at[rel, :, pl.ds(0, size)], xs.at[i], xr.at[i], peer)
        )

    def zcopy(a, j, piece, to, slot):
        here = got[a].at[j, pl.ds(pl.multiple_of(piece * PIECE, 16), PIECE), :]
        return pltpu.make_async_remote_copy(
            src_ref=here, dst_ref=here,
            send_sem=zs.at[2 * a + j, slot], recv_sem=zr.at[2 * a + j, piece],
            device_id={"tensor": to}, device_id_type=MESH,
        )

    def zmoves(step):
        down, up = plane + step, plane - step
        return (
            (down, plane - 1, (plane > 0) & (down < planes), 2 * step),
            (up, plane + 1, (plane < planes - 1) & (up >= 0), 2 * step + 1),
        )

    def spread(a, j):
        directs[2 * j + a].wait_recv()
        for piece, to, has, slot in zmoves(0):
            @pl.when(has)
            def _(piece=piece, to=to, slot=slot):
                zcopy(a, j, piece, to, slot).start()

    def zstep(step, a, js=(0, 1)):
        for j in js:
            for piece, to, has, slot in zmoves(step):
                @pl.when((piece >= 0) & (piece < planes))
                def _(piece=piece):
                    zcopy(a, j, piece, 0, 0).wait_recv()

                if step < planes - 1:
                    @pl.when(has)
                    def _(piece=piece, to=to, slot=slot):
                        zcopy(a, j, piece, to, slot).start()

    def xsent():
        for step in range(planes - 1):
            for piece, to, has, slot in zmoves(step):
                @pl.when(has)
                def _(piece=piece, to=to, slot=slot):
                    for a in (0, 1):
                        for j in (0, 1):
                            zcopy(a, j, piece, to, slot).wait_send()

    ld.wait()
    docs = jnp.broadcast_to(doc_ref[...].astype(F32), (T, T))
    jj = lax.broadcasted_iota(jnp.int32, (T, T), 0)
    ii = lax.broadcasted_iota(jnp.int32, (T, T), 1)
    allowed = (jj <= ii) & (docs == docs.T)
    bias[...] = jnp.where(allowed, 0.0, -jnp.inf).astype(F32)
    lk.wait()
    lq.wait()
    lg.wait()
    row = lax.broadcasted_iota(jnp.int32, (T, HEAD_SIZE), 0).astype(F32)

    def group(kh, _):
        kcols = pl.ds(pl.multiple_of(kh * HEAD_SIZE, HEAD_SIZE), HEAD_SIZE)
        keyg = k[:, kcols]
        total = jnp.zeros((T, HEAD_SIZE), F32)
        for h in range(GROUP):
            cols = pl.ds(pl.multiple_of((kh * GROUP + h) * HEAD_SIZE, HEAD_SIZE), HEAD_SIZE)
            st = lax.dot_general(
                keyg, q[:, cols], (((1,), (1,)), ((), ())), preferred_element_type=F32
            )
            st = st * scale + bias[...]
            e = jnp.exp(st - jnp.max(st, axis=0, keepdims=True))
            p = (e * (1.0 / jnp.sum(e, axis=0, keepdims=True))).astype(BF16)
            pt[kh * GROUP + h] = p
            gm = jnp.where(row < count, g[:, cols].astype(F32), 0.0).astype(BF16)
            total = total + jnp.dot(p, gm, preferred_element_type=F32)
        dv[:, kcols] = (total * count).astype(BF16)
        return 0

    lax.fori_loop(0, kv, group, 0)
    dcopies = [
        remote(dv, dvp, ds.at[0], dr.at[0], peer),
        remote(dv, dvn.at[1, 0], ds.at[1], dr.at[1], same(1)),
    ]
    spread(0, 0)
    spread(1, 0)
    spread(0, 1)
    c0.wait_recv()
    cnts[2] = cnts[0] + cnts[1]
    c1 = remote(cnts.at[2], cnts.at[3], cs.at[1], cr.at[1], same(1))
    lx.wait()
    for c in xcopies:
        c.wait_recv()
    dcopies[0].wait_recv()
    step = 256

    def partial(rel, first, size, store):
        base = same(rel) * R

        def body(t, _):
            off = pl.multiple_of(first + t * step, step)
            xa = x[:, pl.ds(pl.multiple_of(base + off, step), step)]
            xb = xp[rel, :, pl.ds(off, step)]
            store(off, dot_tt(xa, dv[...]) + dot_tt(xb, dvp[...]))
            return 0

        lax.fori_loop(0, size // step, body, 0)

    def send_block(slot, first, size, i, to):
        here = pl.ds(first, size)
        return remote(
            sendbuf.at[slot, here], recvbuf.at[slot, here], ss.at[i], sr.at[i], same(to)
        )

    def fill(slot, rel, first, size, add=None):
        def put(off, val):
            here = pl.ds(off, step)
            if add is not None:
                val = val + recvbuf[add, here, :].astype(F32)
            sendbuf[slot, here, :] = val.astype(BF16)

        partial(rel, first, size, put)

    def keep(off, val):
        acc[pl.ds(off, step), :] = val

    def value_part(rel, size, first=False):
        cols = pl.ds(pl.multiple_of(same(rel) * R, R), size)
        wpart = wg[rel, pl.ds(0, size), :]
        a = jnp.dot(x[:, cols], wpart, preferred_element_type=F32)
        b = jnp.dot(xp[rel, :, pl.ds(0, size)], wpart, preferred_element_type=F32)
        if first:
            vown[...] = a
            vsend[...] = b
        else:
            vown[...] += a
            vsend[...] += b

    late = jnp.where(plane < planes // 2, T - PIECE, 0)
    early = jnp.where(plane < planes // 2, 0, PIECE)
    goes = (
        pl.ds(pl.multiple_of(early, 16), T - PIECE),
        pl.ds(pl.multiple_of(late, 16), PIECE),
    )
    pcopies, qcopies = {}, {}

    def partial_value(a, go):
        here = goes[go]
        i = 2 * go + a
        wpart = wg[0, pl.ds(*spans[a]), :]
        pf[a, 1, here, :] = jnp.dot(got[a][1, here, :], wpart, preferred_element_type=F32)
        pcopies[i] = remote(pf.at[a, 1, here, :], pfr.at[a, here, :], fs.at[i], fr.at[i], peer)
        pf[a, 0, here, :] = jnp.dot(got[a][0, here, :], wpart, preferred_element_type=F32)

    def return_value(a, go):
        here = goes[go]
        i = 2 * go + a
        pcopies[i].wait_recv()
        val = pf[a, 0, here, :] + pfr[a, here, :]
        if a:
            qcopies[2 * go].wait_recv()
            val = val + pr[0, here, :].astype(F32)
        ps[a, here, :] = val.astype(BF16)
        qcopies[i] = remote(
            ps.at[a, here, :], pr.at[a, here, :], qs.at[i], qr.at[i], same(1 if a else 2)
        )

    scopies = []
    for i in range(S // step):
        fill(0, 3, i * step, step)
        scopies.append(send_block(0, i * step, step, i, 1))

    def merge(i):
        scopies[i].wait_recv()
        fill(1, 2, i * step, step, add=0)
        scopies.append(send_block(1, i * step, step, 4 + i, 2))

    zstep(1, 0, (0,))
    spread(1, 1)
    zstep(1, 0, (1,))
    fill(1, 2, S, R - S)
    scopies.append(send_block(1, S, R - S, 3, 2))
    partial(0, 0, S, keep)
    zstep(1, 1, (0,))
    w0.wait_recv()
    w2 = remote(wg.at[2, upper], wg.at[3, upper], ws.at[2], wr.at[2], same(1))
    dcopies[1].wait_recv()
    dcopies.append(remote(dvn.at[1, 0], dvn.at[0, 0], ds.at[2], dr.at[2], same(2)))
    dcopies.append(remote(dvn.at[1, 0], dvn.at[1, 1], ds.at[3], dr.at[3], peer))
    zstep(2, 0)
    partial_value(0, 0)
    zstep(1, 1, (1,))
    return_value(0, 0)
    merge(0)
    zstep(3, 0)
    partial_value(0, 1)
    zstep(2, 1, (0,))
    return_value(0, 1)
    merge(1)
    c1.wait_recv()
    cnts[4] = cnts[2] + cnts[3]
    c2 = remote(cnts.at[4], cnts.at[5], cs.at[2], cr.at[2], same(2))
    merge(2)
    zstep(2, 1, (1,))
    partial_value(1, 0)
    partial(0, S, R - S, keep)
    value_part(0, R, True)
    return_value(1, 0)
    w1.wait_recv()
    value_part(2, R)
    dcopies[2].wait_recv()
    dcopies.append(remote(dvn.at[0, 0], dvn.at[0, 1], ds.at[4], dr.at[4], peer))

    def neighbour_part(a):
        dcopies[4 - a].wait_recv()
        for i in range(spans[a][1] // step):
            cols = pl.ds(i * step, step)
            here = pl.ds(spans[a][0] + i * step, step)
            acc[here, :] += dot_tt(got[a][0, :, cols], dvn[a, 0]) + dot_tt(
                got[a][1, :, cols], dvn[a, 1]
            )

    neighbour_part(0)
    zstep(3, 1)
    partial_value(1, 1)
    vcopy = pltpu.make_async_remote_copy(
        src_ref=vsend, dst_ref=vrecv, send_sem=vs, recv_sem=vr,
        device_id={"dp": peer}, device_id_type=MESH,
    )

    def end_value():
        w2.wait_recv()
        value_part(3, S)
        vcopy.start()

    @pl.when(core == 1)
    def _():
        end_value()

    return_value(1, 1)

    @pl.when(core == 0)
    def _():
        end_value()

    neighbour_part(1)
    vcopy.wait_recv()
    vown[...] += vrecv[...]
    c2.wait_recv()
    inv = 1.0 / (cnts[4] + cnts[5])[0:1, 0:1]
    def contexts(first, count):
        rows = pl.ds(first, count)

        def body(kh, _):
            kcols = pl.ds(pl.multiple_of(kh * HEAD_SIZE, HEAD_SIZE), HEAD_SIZE)
            val = vown[:, kcols].astype(BF16)
            for h in range(GROUP):
                head = kh * GROUP + h
                cols = pl.ds(pl.multiple_of(head * HEAD_SIZE, HEAD_SIZE), HEAD_SIZE)
                ctx[rows, cols] = dot_tt(pt[head, :, rows], val).astype(BF16)
            return 0

        lax.fori_loop(0, kv, body, 0)

    def add_values(go):
        qcopies[2 * go + 1].wait_recv()
        vown[goes[go], :] += pr[1, goes[go], :].astype(F32)

    add_values(0)

    @pl.when(plane < planes // 2)
    def _():
        contexts(0, T // 2)

    def finish(i, first, size):
        scopies[i].wait_recv()
        here = pl.ds(first, size)
        dw_ref[here, :] = (acc[here, :] + recvbuf[1, here, :].astype(F32)) * inv

    finish(3, S, R - S)
    finish(4, 0, step)
    finish(5, step, step)
    add_values(1)

    @pl.when(plane >= planes // 2)
    def _():
        contexts(0, T // 2)

    contexts(T // 2, T // 2)

    finish(6, 2 * step, step)
    xsent()
    partials = list(pcopies.values()) + list(qcopies.values())
    waits = swaps + directs + xcopies + dcopies + scopies + partials
    for c in [w0, w1, w2, vcopy, c0, c1, c2] + waits:
        c.wait_send()


def write_kernel(ctx, dw, ctx_hbm, dw_hbm, sems):
    copies = []
    for src, dst in ((ctx, ctx_hbm), (dw, dw_hbm)):
        rows = src.shape[0] // 2
        for part in range(2):
            here = pl.ds(part * rows, rows)
            copies.append(
                pltpu.make_async_copy(src.at[here], dst.at[here], sems.at[len(copies)])
            )
    for c in copies:
        c.start()
    for c in copies:
        c.wait()


def fused(planes, hidden_in, queries, keys, value_weight, context_grad, doc_ids, token_counts):
    T, M = hidden_in.shape
    C = keys.shape[1]
    Q = queries.shape[1]
    R = value_weight.shape[0]
    heads = Q // HEAD_SIZE
    hbm = pl.BlockSpec(memory_space=pltpu.HBM)
    dma = pltpu.SemaphoreType.DMA
    pinned = [
        pltpu.with_memory_space_constraint(a, pltpu.HBM)
        for a in (hidden_in, queries, keys, value_weight, context_grad, doc_ids)
    ]
    results = tuple(
        pl.pallas_call(
            fused_kernel,
            out_shape=(
                jax.ShapeDtypeStruct((T, Q), BF16),
                jax.ShapeDtypeStruct((R, C), F32),
            ),
            in_specs=[hbm] * 6 + [pl.BlockSpec(memory_space=pltpu.SMEM)],
            out_specs=(pl.BlockSpec(memory_space=pltpu.VMEM),) * 2,
            scratch_shapes=[
                pltpu.VMEM((T, M), BF16),
                pltpu.VMEM((4, T, R), BF16),
                pltpu.VMEM((2, PIECE, R // 4), BF16),
                pltpu.VMEM((2, PIECE, R), BF16),
                pltpu.VMEM((PIECE, R // 4), BF16),
                pltpu.VMEM((PIECE, R), BF16),
                pltpu.VMEM((T, Q), BF16),
                pltpu.VMEM((T, C), BF16),
                pltpu.VMEM((T, Q), BF16),
                pltpu.VMEM((4, R, C), BF16),
                pltpu.VMEM((heads, T, T), BF16),
                pltpu.VMEM((T, T), F32),
                pltpu.VMEM((T, C), BF16),
                pltpu.VMEM((T, C), BF16),
                pltpu.VMEM((2, 2, T, C), BF16),
                pltpu.VMEM((2, T, R // 4), BF16),
                pltpu.VMEM((2, T, R), BF16),
                pltpu.VMEM((T, C), F32),
                pltpu.VMEM((T, C), F32),
                pltpu.VMEM((T, C), F32),
                pltpu.VMEM((2, 2, T, C), F32),
                pltpu.VMEM((2, T, C), F32),
                pltpu.VMEM((2, T, C), BF16),
                pltpu.VMEM((2, T, C), BF16),
                pltpu.VMEM((2, R, C), BF16),
                pltpu.VMEM((2, R, C), BF16),
                pltpu.VMEM((R, C), F32),
                pltpu.VMEM((6, 8, 128), F32),
                pltpu.VMEM(doc_ids.shape, jnp.int32),
                dma((10,)),
                dma((4,)), dma((4,)),
                dma((4,)), dma((4,)),
                dma((3,)), dma((3,)),
                dma((5,)), dma((5,)),
                dma, dma,
                dma((7,)), dma((7,)),
                dma((4,)), dma((4,)),
                dma((4, 2 * (planes - 1))), dma((4, planes)),
                dma((4,)), dma((4,)),
                dma((4,)), dma((4,)),
                dma((2,)), dma((2,)),
            ],
            compiler_params=pltpu.CompilerParams(
                collective_id=0, has_side_effects=True, vmem_limit_bytes=48 * 1024 * 1024
            ),
        )(*pinned, token_counts)
    )
    return tuple(
        pl.pallas_call(
            write_kernel,
            out_shape=tuple(jax.ShapeDtypeStruct(a.shape, a.dtype) for a in results),
            in_specs=[pl.BlockSpec(memory_space=pltpu.VMEM)] * 2,
            out_specs=(hbm, hbm),
            scratch_shapes=[dma((4,))],
        )(*(pltpu.with_memory_space_constraint(a, pltpu.VMEM) for a in results))
    )


def solution(mesh):
    in_specs = (
        P("dp", None),
        P("dp", "tensor"),
        P("dp", "tensor"),
        P("dp", "tensor"),
        P("dp", "tensor"),
        P("dp", None),
        P("dp"),
    )
    out_specs = (P("dp", "tensor"), P("dp", "tensor"))
    planes = mesh.shape["tensor"]
    small = (mesh.shape["dp"], planes) == (8, 4)
    body = functools.partial(fused, planes) if small else plain
    return jax.shard_map(body, mesh=mesh, in_specs=in_specs, out_specs=out_specs, check_vma=False)
```
